512 devices in a mesh: dp: 16 (over x, y), heads: 16 (over z), side: 2 (over core).
Axes of the slice: x: 4, y: 4, z: 16, core: 2. Of those that a mesh axis runs over, the one named last changes fastest.
Arguments:
- queries: bfloat16 [384, 2, 4096], P('dp', None, ('heads', 'side')), may hold values from -6 to 6
- new_keys: bfloat16 [384, 2, 4096], P('dp', None, ('heads', 'side')), may hold values from -6 to 6
- new_values: bfloat16 [384, 2, 4096], P('dp', None, ('heads', 'side')), may hold values from -6 to 6
- head_states: bfloat16 [384, 32, 128, 128], P('dp', ('heads', 'side')), may hold values from -6 to 6
- slopes: float32 [32], P(('heads', 'side')), may hold values from 0.004 to 0.9
- head_gain: float32 [4096], P(('heads', 'side')), may hold values from 0.5 to 1.5
- out_weight: bfloat16 [4096, 3072], P(('heads', 'side')), may hold values from -0.1875 to 0.1875
- residual: bfloat16 [384, 2, 3072], P('dp', None, ('heads', 'side')), may hold values from -10 to 10
- norm_gain: float32 [3072], replicated, may hold values from 0.5 to 1.5
- expert_ids: int32 [384, 2, 2], P('dp'), may hold values from 0 to 15, all different within a row; in each aligned block of 48 rows (0 to 47, 48 to 95, ..., all dimensions but the last counted through in order) at most 9 rows name the same one
- expert_gates: float32 [384, 2, 2], P('dp'), may hold values from 0.2 to 1
- w_gate: bfloat16 [16, 16, 192, 4608], P('dp', None, 'side', 'heads'), may hold values from -0.109375 to 0.109375
- w_up: bfloat16 [16, 16, 192, 4608], P('dp', None, 'side', 'heads'), may hold values from -0.109375 to 0.109375
- w_down: bfloat16 [16, 4608, 16, 192], P('dp', 'heads', None, 'side'), may hold values from -0.125 to 0.125
Outputs:
- state_out: bfloat16 [384, 32, 128, 128], P('dp', ('heads', 'side'))
- resid_out: bfloat16 [384, 2, 3072], P('dp', None, ('heads', 'side'))
- moe_out: bfloat16 [384, 2, 3072], P('dp', None, ('heads', 'side'))
The draws below stay inside these ranges and needn't reach their ends.
Inputs may be any that keep to these rules, and one draw needn't show every extreme that they name: `expert_ids`: among the 48 tokens of one dp index a token's 2 experts differ, no expert is chosen by more than 9 of them, and some expert is chosen by exactly 9.
All inputs are finite; a program needn't handle non-finite values.
Results may differ from the reference program's by a relative error of at most 0.025.
Values may be sent and summed in bfloat16 or wider, within the bound.
A program may use at most 64 MiB of HBM per device.

```python
import math
import jax
import jax.numpy as jnp
import numpy as np
from jax import lax

D = 3072
HEADS = 32
HEAD = 128
FF = 4608
TOP = 2
STEPS = 2
REQUESTS = 384
EXPERTS = 16
D_GROUP = 192
T_DEV = 48
CAP = 9
N_DP = 16
N_HEADS = 16


def draw_residual(key, part):
    first_key = jax.random.fold_in(key, 0)
    columns = jnp.arange(D, dtype=jnp.float32) / D
    raw_values = jnp.clip(jax.random.normal(first_key, (REQUESTS, STEPS, D), jnp.float32), -5.0, 5.0)
    col_scale = 0.2 * jnp.exp(math.log(10.0) * columns)
    return (raw_values * col_scale).astype(jnp.bfloat16)


def strengthened(values, key, source, target, blocks, factor):
    owner, partner = [(jnp.arange(values.shape[axis_at]) // (values.shape[axis_at] // blocks)).reshape([-1 if axis == axis_at else 1 for axis in range(values.ndim)]) for axis_at in (source, target)]
    chosen = jax.random.permutation(key, blocks)[partner]
    strong = (owner == chosen) | (owner == (partner + blocks // 2) % blocks)
    return jnp.where(strong, factor * values, values)


def block_scale(key, dims, pieces, smallest, largest):
    level, own = 1.0, jax.random.fold_in(key, 6)
    for position, parts in pieces:
        heights = jnp.exp(jax.random.uniform(jax.random.fold_in(own, position), (parts,), jnp.float32, smallest / len(pieces), largest / len(pieces)))
        level = level * jnp.repeat(heights, dims[position] // parts).reshape([-1 if axis == position else 1 for axis in range(len(dims))])
    return level


def shared_out(rng, own, number, rows, number_of, top, bound, slope):
    ranking = jax.random.permutation(rng, number_of)
    crowded, common = shares(number_of, rows * top, bound, slope, True), shares(number_of, rows * top, bound, slope, False)
    places = jnp.arange(number_of)

    def named(lengths, offset_by):
        used = int((lengths > 0).sum())
        fixed = max(1, used // 4)
        shifted = fixed + (places - fixed + offset_by * (used - fixed)) % max(1, number_of - fixed)
        return jnp.zeros((number_of,), jnp.int32).at[ranking[jnp.where(places < fixed, places, shifted)]].set(jnp.asarray(lengths, jnp.int32))

    lengths = jnp.where(number % 4 == 0, named(crowded, number // 4), named(common, number - number // 4 - 1))
    mixed = jax.random.permutation(jax.random.fold_in(own, 3), number_of)
    donor, sink = mixed[0:number_of // 2 * 2:2], mixed[1:number_of // 2 * 2:2]
    room = jnp.minimum(lengths[donor] - 1, bound - lengths[sink]) // 2
    room = jnp.where((donor == ranking[0]) | (sink == ranking[0]) | (lengths[sink] == 0), 0, jnp.maximum(room, 0))
    shifted = jax.random.randint(jax.random.fold_in(own, 4), (number_of // 2,), 0, 1 << 20) % (room + 1)
    lengths = lengths.at[donor].add(-shifted).at[sink].add(shifted)
    labels = jnp.searchsorted(jnp.cumsum(lengths), jnp.arange(rows * top), side="right").astype(jnp.int32)
    table = labels.reshape(top, rows).T
    table = table[jax.random.permutation(jax.random.fold_in(own, 1), rows)]
    offset_by = jax.random.randint(jax.random.fold_in(own, 2), (rows, 1), 0, top)
    return jnp.take_along_axis(table, (jnp.arange(top)[None, :] + offset_by) % top, axis=1)


def shares(amount, total, limit, lean, full):
    portions = [(1 << 20) // math.isqrt(grade ** lean) + 1 for grade in range(1, amount + 1)]
    largest = limit if full else min(limit, max(-(-total // amount), total * portions[0] // sum(portions)))
    least = 1 if total - largest >= amount - 1 else 0
    holding, surplus = [largest] + [least] * (amount - 1), total - largest - least * (amount - 1)
    while surplus > 0:
        movable = [i for i in range(1, amount) if holding[i] < largest] or [i for i in range(1, amount) if holding[i] < limit]
        mass, budget = sum([portions[i] for i in movable]), surplus
        for i in movable:
            addition = min(limit - holding[i], max(1, budget * portions[i] // mass), surplus)
            holding[i] = holding[i] + addition
            surplus = surplus - addition
    return np.array(holding)


def scatter_about(stream_key, dims, deviation, bound, shards=(), kind=jnp.bfloat16):
    level = block_scale(stream_key, dims, shards, -0.22, 0.18) if shards else 1.0
    drawn = jax.random.normal(stream_key, dims, jnp.float32) * deviation * level
    return jnp.minimum(jnp.maximum(drawn, -bound), bound).astype(kind)


def bell_draw_with(stream_key, shape, scale, limit, cuts, heavy, kind=jnp.bfloat16):
    entries = scale * jax.random.normal(stream_key, shape, jnp.float32)
    if cuts:
        entries = entries * block_scale(stream_key, shape, cuts, -0.22, 0.18)
    return jnp.clip(strengthened(entries, jax.random.fold_in(stream_key, 3), *heavy), -limit, limit).astype(kind)


def setup_inputs(seed: int = 0) -> dict:
    key_list = jax.random.split(jax.random.key(seed), 15)
    queries = scatter_about(key_list[0], (REQUESTS, STEPS, HEADS * HEAD), 1.0, 6.0, ((0, 16), (2, 32)))
    new_keys = scatter_about(key_list[1], (REQUESTS, STEPS, HEADS * HEAD), 1.0, 6.0, ((0, 16), (2, 32)))
    new_values = scatter_about(key_list[2], (REQUESTS, STEPS, HEADS * HEAD), 1.0, 6.0, ((0, 16), (2, 32)))
    head_states = scatter_about(key_list[3], (REQUESTS, HEADS, HEAD, HEAD), 1.0, 6.0, ((0, 16), (1, 32)))
    slopes = jnp.clip(jnp.exp(math.log(0.9) - 5.4161003 * jax.random.uniform(key_list[4], (HEADS,), jnp.float32) ** block_scale(key_list[4], (HEADS,), ((0, 32),), -0.2, 0.2)), 0.004, 0.9)
    head_gain = jnp.clip(1.0 + 0.1 * jax.random.normal(key_list[5], (HEADS * HEAD,), jnp.float32), 0.5, 1.5)
    out_weight = bell_draw_with(key_list[6], (HEADS * HEAD, D), (HEADS * HEAD) ** -0.5, 0.1875, ((0, 32),), (0, 1, 32, 2.75))
    residual = draw_residual(jax.random.fold_in(key_list[14], 71), 0)
    norm_gain = jnp.clip(1.0 + 0.1 * jax.random.normal(key_list[8], (D,), jnp.float32), 0.5, 1.5)
    expert_ids_keys = jax.random.split(jax.random.fold_in(key_list[9], 1), REQUESTS * STEPS // T_DEV)
    expert_ids_turns = jax.random.permutation(jax.random.fold_in(key_list[9], 3), REQUESTS * STEPS // T_DEV)
    expert_ids = jax.vmap(lambda own, number: shared_out(jax.random.fold_in(key_list[9], 2), own, number, T_DEV, EXPERTS, TOP, CAP, 2))(expert_ids_keys, expert_ids_turns).reshape((REQUESTS, STEPS, TOP))
    expert_gates = jnp.clip(jnp.exp(math.log(1.0) - 1.609438 * jax.random.uniform(key_list[10], (REQUESTS, STEPS, TOP), jnp.float32) ** block_scale(key_list[10], (REQUESTS, STEPS, TOP), ((0, 16),), -0.2, 0.2)), 0.2, 1.0)
    w_gate = scatter_about(key_list[11], (EXPERTS, N_HEADS, D_GROUP, FF), D ** -0.5, 0.109375, ((0, 16), (2, 2), (3, 16)))
    w_up = scatter_about(key_list[12], (EXPERTS, N_HEADS, D_GROUP, FF), D ** -0.5, 0.109375, ((0, 16), (2, 2), (3, 16)))
    w_down = bell_draw_with(key_list[13], (EXPERTS, FF, N_HEADS, D_GROUP), FF ** -0.5, 0.125, ((0, 16), (1, 16), (3, 2)), (1, 2, 16, 2.0))
    return {"queries": queries, "new_keys": new_keys, "new_values": new_values, "head_states": head_states, "slopes": slopes, "head_gain": head_gain, "out_weight": out_weight, "residual": residual, "norm_gain": norm_gain, "expert_ids": expert_ids, "expert_gates": expert_gates, "w_gate": w_gate, "w_up": w_up, "w_down": w_down}


def reference(queries, new_keys, new_values, head_states, slopes, head_gain, out_weight, residual, norm_gain, expert_ids, expert_gates, w_gate, w_up, w_down):
    query_rows = queries.astype(jnp.float32).reshape(REQUESTS, STEPS, HEADS, HEAD)
    key_rows = new_keys.astype(jnp.float32).reshape(REQUESTS, STEPS, HEADS, HEAD)
    value_rows = new_values.astype(jnp.float32).reshape(REQUESTS, STEPS, HEADS, HEAD)
    decays = jnp.exp(-slopes)[None, :, None, None]
    current = head_states.astype(jnp.float32)
    outputs = []
    for step in range(STEPS):
        current = decays * current + key_rows[:, step, :, :, None] * value_rows[:, step, :, None, :]
        outputs.append(jnp.einsum('rhi,rhij->rhj', query_rows[:, step], current, precision=lax.Precision.HIGHEST))
    state_out = current.astype(jnp.bfloat16)
    head_output = jnp.stack(outputs, 1)
    scaled = head_output * lax.rsqrt(lax.optimization_barrier(jnp.mean(head_output * head_output, -1, keepdims=True)) + 1e-06)
    normed = (scaled * head_gain.reshape(HEADS, HEAD)).astype(jnp.bfloat16).reshape(REQUESTS * STEPS, HEADS * HEAD)
    projected = jnp.dot(normed, out_weight, preferred_element_type=jnp.float32)
    resid_out = (residual.reshape(REQUESTS * STEPS, D).astype(jnp.float32) + projected).astype(jnp.bfloat16)
    stream = resid_out.astype(jnp.float32)
    mixed_in = (stream * lax.rsqrt(lax.optimization_barrier(jnp.mean(stream * stream, 1, keepdims=True)) + 1e-06) * norm_gain).astype(jnp.bfloat16)
    flat_ids = expert_ids.reshape(-1)
    token_index = jnp.arange(REQUESTS * STEPS * TOP, dtype=jnp.int32) // TOP
    most_rows = N_DP * CAP

    def one_expert(expert):
        chosen = flat_ids == expert
        ordering = jnp.argsort(jnp.where(chosen, 0, 1).astype(jnp.int32), stable=True)[:most_rows].astype(jnp.int32)
        inputs = mixed_in[token_index[ordering]]
        gate_matrix = w_gate[expert].reshape(D, FF)
        up_matrix = w_up[expert].reshape(D, FF)
        down_matrix = w_down[expert].reshape(FF, D)
        gate_val = jnp.dot(inputs, gate_matrix, preferred_element_type=jnp.float32)
        up_val = jnp.dot(inputs, up_matrix, preferred_element_type=jnp.float32)
        activation = (jax.nn.silu(gate_val) * up_val).astype(jnp.bfloat16)
        result = jnp.dot(activation, down_matrix, preferred_element_type=jnp.float32).astype(jnp.bfloat16)
        kept = jnp.where(chosen[ordering][:, None], result.astype(jnp.float32), jnp.zeros_like(result, dtype=jnp.float32))
        return (kept, ordering)
    results, orderings = lax.map(one_expert, jnp.arange(EXPERTS, dtype=jnp.int32))
    per_choice = jnp.zeros((REQUESTS * STEPS * TOP, D), jnp.float32).at[orderings.reshape(-1)].add(results.reshape(-1, D))
    weighted = per_choice * expert_gates.reshape(-1)[:, None]
    moe_out = lax.optimization_barrier(jnp.sum(weighted.reshape(REQUESTS * STEPS, TOP, D), 1)).astype(jnp.bfloat16)
    return (state_out, resid_out.reshape(REQUESTS, STEPS, D), moe_out.reshape(REQUESTS, STEPS, D))
```

```python
import functools

import jax
import jax.numpy as jnp
from jax import lax
from jax.experimental import pallas as pl
from jax.experimental.pallas import tpu as pltpu
from jax.sharding import PartitionSpec as P

F32 = jnp.float32
BF16 = jnp.bfloat16
MESH = pl.DeviceIdType.MESH
SLOTS = 8
LANES = 128
IN_NAMES = ("q", "k", "v", "hg", "res", "ng", "ids", "gates", "state", "wo", "wg", "wu", "wd")


def dot(a, b):
    return jnp.dot(a, b, preferred_element_type=F32)


def kernel(dims, *refs):
    (experts, depth, rows_y, requests, steps, top, piece, hidden, width) = dims
    tokens = requests * steps
    feats = depth * piece
    groups = feats // LANES
    row_tiles = tokens // 8
    tiles = groups * row_tiles
    per = -(-tiles // depth)
    n_in = len(IN_NAMES)
    hbm = dict(zip(IN_NAMES, refs[:n_in]))
    slope_ref, state_out, resid_out, moe_out = refs[n_in : n_in + 4]
    vm = dict(zip(IN_NAMES, refs[n_in + 4 : 2 * n_in + 4]))
    (
        wdd, snew, ex_src, ex_dst, part, tsum, rs_buf, disp, dispo, recv, recvo,
        xg, ss_src, ss_dst, gu_src, gu_dst, back, backo, comb, combo, rs2_src, rs2_buf,
        in_sem, st_sem, side_send, side_recv, z_send, z_recv, dp_send, dp_recv,
    ) = refs[2 * n_in + 4 :]

    my_dp = lax.axis_index("dp")
    my_z = lax.axis_index("heads")
    my_side = lax.axis_index("side")
    partner = (my_dp, my_z, 1 - my_side)

    def z_peer(i):
        d = depth // 2 - (i + 1) // 2
        sign = 1 - 2 * ((i + 1) % 2)
        return (my_z + sign * d + depth) % depth

    def dp_peer(i):
        cols = experts // rows_y
        x = (my_dp // rows_y + i // rows_y) % cols
        y = (my_dp % rows_y + i % rows_y) % rows_y
        return x * rows_y + y

    def loads(name):
        i = IN_NAMES.index(name)
        return pltpu.make_async_copy(hbm[name], vm[name], in_sem.at[i])

    for name in ("state", "q", "k", "v", "hg", "wo", "res", "ids", "gates", "ng", "wg", "wu", "wd"):
        loads(name).start()

    barrier = pltpu.get_barrier_semaphore()

    def greet_z(i, c):
        pl.semaphore_signal(barrier, 1, device_id=(my_dp, z_peer(i), my_side), device_id_type=MESH)
        return c

    def greet_dp(i, c):
        pl.semaphore_signal(barrier, 1, device_id=(dp_peer(i), my_z, my_side), device_id_type=MESH)
        return c

    lax.fori_loop(0, depth - 1, greet_z, 0)
    lax.fori_loop(1, experts, greet_dp, 0)
    pl.semaphore_signal(barrier, 1, device_id=partner, device_id_type=MESH)

    for name in ("q", "k", "v", "hg", "state"):
        loads(name).wait()
    decay = jnp.exp(jnp.full((1, LANES), -slope_ref[0], F32))
    q = vm["q"][...].astype(F32)
    k = vm["k"][...].astype(F32)
    v = vm["v"][...].astype(F32)
    q1, q2 = q[:, 0, :], q[:, 1, :]
    k1, k2 = k[:, 0, :], k[:, 1, :]
    v1, v2 = v[:, 0, :], v[:, 1, :]
    read = jnp.einsum(
        "rsi,rij->rsj", vm["q"][...], vm["state"][...].reshape(requests, LANES, LANES),
        preferred_element_type=F32,
    )
    dotted = lambda a, b: jnp.sum(a * b, 1, keepdims=True)
    o1 = decay * read[:, 0, :] + dotted(q1, k1) * v1
    o2 = decay * decay * read[:, 1, :] + decay * (dotted(q2, k1) * v1) + dotted(q2, k2) * v2
    out = jnp.concatenate([o1, o2], 0)
    normed = out * lax.rsqrt(jnp.mean(out * out, 1, keepdims=True) + 1e-6) * vm["hg"][...]
    loads("wo").wait()
    projected = dot(normed.astype(BF16), vm["wo"][...])
    halves = [
        jnp.concatenate(
            [projected[:, (2 * a + s) * piece : (2 * a + s + 1) * piece] for a in range(depth)], 1
        )
        for s in range(2)
    ]
    first = my_side == 0
    ex_src[...] = jnp.where(first, halves[1], halves[0]).astype(BF16)
    own = jnp.where(first, halves[0], halves[1])

    pl.semaphore_wait(barrier, depth + experts - 1)

    def to_partner(src, dst, i):
        return pltpu.make_async_remote_copy(
            src_ref=src, dst_ref=dst, send_sem=side_send.at[i], recv_sem=side_recv.at[i],
            device_id=partner, device_id_type=MESH,
        )

    exchange = to_partner(ex_src, ex_dst, 0)
    exchange.start()

    loads("res").wait()
    res = vm["res"][...].astype(F32)
    res = jnp.concatenate([res[:, s, :] for s in range(steps)], 0).astype(BF16)
    place = (
        lax.broadcasted_iota(jnp.int32, (piece, feats), 1)
        == lax.broadcasted_iota(jnp.int32, (piece, feats), 0) + my_z * piece
    ).astype(BF16)
    own = own + dot(res, place)
    exchange.wait()
    chip = own + ex_dst[...].astype(F32)
    for g in range(groups):
        block = chip[:, g * LANES : (g + 1) * LANES].reshape(row_tiles, 8, LANES)
        part[g * row_tiles : (g + 1) * row_tiles] = block.astype(BF16)
    if per * depth > tiles:
        part[tiles:] = jnp.zeros((per * depth - tiles, 8, LANES), BF16)

    def z_copy(phase, src, dst, i, peer):
        return pltpu.make_async_remote_copy(
            src_ref=src, dst_ref=dst, send_sem=z_send.at[phase, i], recv_sem=z_recv.at[phase, i],
            device_id=(my_dp, peer, my_side), device_id_type=MESH,
        )

    def rs_copy(i):
        peer = z_peer(i)
        return z_copy(0, part.at[pl.ds(peer * per, per)], rs_buf.at[i], i, peer)

    def rs_start(i, c):
        rs_copy(i).start()
        return c

    lax.fori_loop(0, depth - 1, rs_start, 0)

    kd = decay * k1
    kd_hi = kd.astype(BF16).astype(F32)
    lhs = jnp.stack([kd_hi, kd - kd_hi, k2], 1).astype(BF16)
    rhs = jnp.stack([v1, v1, v2], 1).astype(BF16)
    decay2 = decay * decay
    for r in range(requests):
        outer = lax.dot_general(
            lhs[r], rhs[r], (((0,), (0,)), ((), ())), preferred_element_type=F32
        )
        snew[r, 0] = (decay2 * vm["state"][r, 0].astype(F32) + outer).astype(BF16)
    state_copy = pltpu.make_async_copy(snew, state_out, st_sem)
    state_copy.start()

    loads("ids").wait()
    loads("gates").wait()
    row_e = lax.broadcasted_iota(jnp.int32, (experts, requests), 0).astype(F32)
    row_m = lax.broadcasted_iota(jnp.int32, (experts * SLOTS, requests), 0).astype(F32)
    upper = (
        lax.broadcasted_iota(jnp.int32, (requests, requests), 0)
        < lax.broadcasted_iota(jnp.int32, (requests, requests), 1)
    ).astype(BF16)
    taken = jnp.zeros((experts, 1), F32)
    sels, selos, weights, weightos = [], [], [], []
    for s in range(steps):
        sel = jnp.zeros((experts * SLOTS, requests), F32)
        selo = jnp.zeros((experts, requests), F32)
        wsel, wselo = sel, selo
        for c in range(top):
            ids = vm["ids"][s, c : c + 1, :].astype(F32)
            gate = vm["gates"][s, c : c + 1, :]
            onehot = (row_e == ids).astype(F32)
            before = dot(onehot.astype(BF16), upper) + taken
            slot = jnp.sum(onehot * before, 0, keepdims=True)
            taken = taken + jnp.sum(onehot, 1, keepdims=True)
            hit = (row_m == jnp.where(slot < SLOTS, ids * SLOTS + slot, -1.0)).astype(F32)
            hito = (row_e == jnp.where(slot < SLOTS, -1.0, ids)).astype(F32)
            sel, selo = sel + hit, selo + hito
            wsel, wselo = wsel + hit * gate, wselo + hito * gate
        sels.append(sel)
        selos.append(selo)
        weights.append(wsel)
        weightos.append(wselo)
    sel = jnp.concatenate(sels, 1).astype(BF16)
    selo = jnp.concatenate(selos, 1).astype(BF16)
    weight = jnp.concatenate(weights, 1)
    weighto = jnp.concatenate(weightos, 1)

    loads("wd").wait()
    for a in range(depth):
        wdd[:, a * piece : (a + 1) * piece] = vm["wd"][:, a, :]

    def rs_done(i, acc):
        i = depth - 2 - i
        rs_copy(i).wait()
        return acc + rs_buf[i].astype(F32)

    mine = pl.ds(my_z * per, per)
    total = lax.fori_loop(0, depth - 1, rs_done, part[mine].astype(F32))
    tsum[mine] = total.astype(BF16)

    def ag_copy(i, wait=False):
        peer = z_peer(i)
        origin = (2 * my_z - peer + depth) % depth if wait else my_z
        there = tsum.at[pl.ds(origin * per, per)]
        return z_copy(1, there, there, i, peer)

    def ag_start(i, c):
        ag_copy(i).start()
        return c

    def ag_done(i, c):
        i = depth - 2 - i
        ag_copy(i).wait_send()
        ag_copy(i, True).wait_recv()
        return c

    lax.fori_loop(0, depth - 1, ag_start, 0)
    loads("ng").wait()
    gain = jnp.concatenate(
        [
            jnp.where(
                first,
                vm["ng"][:, 2 * a * piece : (2 * a + 1) * piece],
                vm["ng"][:, (2 * a + 1) * piece : (2 * a + 2) * piece],
            )
            for a in range(depth)
        ],
        1,
    )
    lax.fori_loop(0, depth - 1, ag_done, 0)

    cols = []
    for g in range(groups):
        block = tsum[g * row_tiles : (g + 1) * row_tiles].astype(F32)
        cols.append(block.reshape(tokens, LANES).astype(BF16))
    stream = jnp.concatenate(cols, 1)
    disp[...] = dot(sel, stream).reshape(experts, SLOTS, feats).astype(BF16)
    over = dot(selo, stream)
    for e in range(experts):
        dispo[e] = over[e : e + 1]

    def dp_copy(phase, src, dst, i, peer):
        return pltpu.make_async_remote_copy(
            src_ref=src, dst_ref=dst, send_sem=dp_send.at[phase, i], recv_sem=dp_recv.at[phase, i],
            device_id=(peer, my_z, my_side), device_id_type=MESH,
        )

    def go_copies(i):
        peer = dp_peer(i)
        return (
            dp_copy(0, disp.at[peer], recv.at[i], i, peer),
            dp_copy(1, dispo.at[peer], recvo.at[i], i, peer),
        )

    def go_start(i, c):
        for copy in go_copies(i):
            copy.start()
        return c

    def go_done(i, c):
        for copy in go_copies(i):
            copy.wait()
        return c

    lax.fori_loop(1, experts, go_start, 0)
    recv[0] = disp[my_dp]
    recvo[0] = dispo[my_dp]
    resid_out[...] = lax.dot_general(
        stream, place, (((1,), (1,)), ((), ())), preferred_element_type=F32
    ).astype(BF16)
    loads("wg").wait()
    loads("wu").wait()
    lax.fori_loop(1, experts, go_done, 0)

    main = experts * SLOTS
    slots = main + experts
    for j in range(experts // 2 + experts // 16 + (1 if experts % 16 else 0)):
        lo = 16 * j
        if lo < main:
            x = recv[2 * j : 2 * j + 2].astype(F32).reshape(16, feats)
            n = 16
        else:
            x = jnp.concatenate([recvo[e] for e in range(experts)], 0)
            n = experts
        squares = jnp.sum(x * x, 1, keepdims=True)
        ss_src[lo : lo + n, :] = jnp.broadcast_to(squares, (n, LANES))
        xg[lo : lo + n, :] = (x * gain).astype(BF16)
    gate_own = dot(xg[...], vm["wg"][...].reshape(feats, hidden))
    gu_src[0] = gate_own.astype(BF16)
    up_own = dot(xg[...], vm["wu"][...].reshape(feats, hidden))
    gu_src[1] = up_own.astype(BF16)
    gu_copy = to_partner(gu_src, gu_dst, 1)
    ss_copy = to_partner(ss_src, ss_dst, 2)
    gu_copy.start()
    ss_copy.start()
    gu_copy.wait()
    ss_copy.wait()
    scale = lax.rsqrt((ss_src[...] + ss_dst[...]) / width + 1e-6)[:, :1]
    gate_val = (gate_own + gu_dst[0].astype(F32)) * scale
    up_val = (up_own + gu_dst[1].astype(F32)) * scale
    act = (gate_val / (1.0 + jnp.exp(-gate_val)) * up_val).astype(BF16)

    down = dot(act, wdd[...])
    back[...] = down[:main].reshape(experts, SLOTS, feats).astype(BF16)
    for e in range(experts):
        backo[e] = down[main + e : main + e + 1]

    def home(i):
        cols = experts // rows_y
        x = (my_dp // rows_y - i // rows_y + cols) % cols
        y = (my_dp % rows_y - i % rows_y + rows_y) % rows_y
        return x * rows_y + y

    def back_copies(i, wait=False):
        peer = home(i)
        slot = dp_peer(i) if wait else my_dp
        return (
            dp_copy(2, back.at[i], comb.at[slot], i, peer),
            dp_copy(3, backo.at[i], combo.at[slot], i, peer),
        )

    def back_start(i, c):
        for copy in back_copies(i):
            copy.start()
        return c

    def back_done(i, c):
        for copy in back_copies(i):
            copy.wait_send()
        for copy in back_copies(i, True):
            copy.wait_recv()
        return c

    lax.fori_loop(1, experts, back_start, 0)
    comb[my_dp] = back[0]
    combo[my_dp] = backo[0]
    w_hi = weight.astype(BF16)
    w_lo = (weight - w_hi.astype(F32)).astype(BF16)
    lax.fori_loop(1, experts, back_done, 0)

    tdot = lambda a, b: lax.dot_general(a, b, (((0,), (0,)), ((), ())), preferred_element_type=F32)
    got = comb[...].astype(F32).reshape(main, feats).astype(BF16)
    goto = jnp.concatenate([combo[e] for e in range(experts)], 0).astype(BF16)
    mixed = tdot(w_hi, got) + tdot(w_lo, got) + tdot(weighto.astype(BF16), goto)

    for a in range(depth):
        rs2_src[a] = mixed[:, a * piece : (a + 1) * piece].astype(BF16)

    def rs2_copy(i):
        peer = z_peer(i)
        return z_copy(2, rs2_src.at[peer], rs2_buf.at[i], i, peer)

    def rs2_start(i, c):
        rs2_copy(i).start()
        return c

    def rs2_done(i, acc):
        i = depth - 2 - i
        rs2_copy(i).wait()
        return acc + rs2_buf[i].astype(F32)

    lax.fori_loop(0, depth - 1, rs2_start, 0)
    final = lax.fori_loop(0, depth - 1, rs2_done, rs2_src[my_z].astype(F32))
    moe_out[...] = final.astype(BF16)
    state_copy.wait()


def layer(mesh_shape, q, k, v, state, slopes, hg, wo, res, ng, ids, gates, wg, wu, wd):
    experts, depth = mesh_shape["dp"], mesh_shape["heads"]
    requests, steps, head = q.shape
    piece = res.shape[2]
    hidden = wg.shape[3]
    top = ids.shape[2]
    width = ng.shape[0]
    tokens = requests * steps
    feats = depth * piece
    per = -(-(feats // LANES) * (tokens // 8) // depth)
    main = experts * SLOTS
    slots = main + experts
    rows_y = 4 if experts == 16 else experts
    dims = (experts, depth, rows_y, requests, steps, top, piece, hidden, width)
    operands = {
        "q": q, "k": k, "v": v, "hg": hg.reshape(1, head), "res": res, "ng": ng.reshape(1, width),
        "ids": ids.transpose(1, 2, 0), "gates": gates.transpose(1, 2, 0), "state": state, "wo": wo,
        "wg": wg[0], "wu": wu[0], "wd": wd[0],
    }
    arrays = [operands[name] for name in IN_NAMES]
    dma = pltpu.SemaphoreType.DMA
    scratch = [pltpu.VMEM(a.shape, a.dtype) for a in arrays] + [
        pltpu.VMEM((hidden, feats), BF16),
        pltpu.VMEM(state.shape, BF16),
        pltpu.VMEM((tokens, feats), BF16),
        pltpu.VMEM((tokens, feats), BF16),
        pltpu.VMEM((per * depth, 8, LANES), BF16),
        pltpu.VMEM((per * depth, 8, LANES), BF16),
        pltpu.VMEM((depth - 1, per, 8, LANES), BF16),
        pltpu.VMEM((experts, SLOTS, feats), BF16),
        pltpu.VMEM((experts, 1, feats), F32),
        pltpu.VMEM((experts, SLOTS, feats), BF16),
        pltpu.VMEM((experts, 1, feats), F32),
        pltpu.VMEM((slots, feats), BF16),
        pltpu.VMEM((slots, LANES), F32),
        pltpu.VMEM((slots, LANES), F32),
        pltpu.VMEM((2, slots, hidden), BF16),
        pltpu.VMEM((2, slots, hidden), BF16),
        pltpu.VMEM((experts, SLOTS, feats), BF16),
        pltpu.VMEM((experts, 1, feats), F32),
        pltpu.VMEM((experts, SLOTS, feats), BF16),
        pltpu.VMEM((experts, 1, feats), F32),
        pltpu.VMEM((depth, tokens, piece), BF16),
        pltpu.VMEM((depth - 1, tokens, piece), BF16),
        dma((len(IN_NAMES),)),
        dma,
        dma((3,)),
        dma((3,)),
        dma((3, depth)),
        dma((3, depth)),
        dma((4, experts)),
        dma((4, experts)),
    ]
    any_spec = pl.BlockSpec(memory_space=pl.ANY)
    state_new, resid, moe = pl.pallas_call(
        functools.partial(kernel, dims),
        out_shape=(
            jax.ShapeDtypeStruct(state.shape, BF16),
            jax.ShapeDtypeStruct((tokens, piece), BF16),
            jax.ShapeDtypeStruct((tokens, piece), BF16),
        ),
        in_specs=[any_spec] * len(arrays) + [pl.BlockSpec(memory_space=pltpu.SMEM)],
        out_specs=(
            any_spec,
            pl.BlockSpec(memory_space=pltpu.VMEM),
            pl.BlockSpec(memory_space=pltpu.VMEM),
        ),
        scratch_shapes=scratch,
        compiler_params=pltpu.CompilerParams(
            collective_id=0, has_side_effects=True, vmem_limit_bytes=56 * 1024 * 1024
        ),
        name="layer",
    )(*arrays, slopes)
    back = lambda x: x.reshape(steps, requests, piece).transpose(1, 0, 2)
    return state_new, back(resid), back(moe)


def solution(mesh):
    return jax.shard_map(
        functools.partial(layer, dict(mesh.shape)),
        mesh=mesh,
        in_specs=(
            P("dp", None, ("heads", "side")),
            P("dp", None, ("heads", "side")),
            P("dp", None, ("heads", "side")),
            P("dp", ("heads", "side"), None, None),
            P(("heads", "side")),
            P(("heads", "side")),
            P(("heads", "side"), None),
            P("dp", None, ("heads", "side")),
            P(),
            P("dp", None, None),
            P("dp", None, None),
            P("dp", None, "side", "heads"),
            P("dp", None, "side", "heads"),
            P("dp", "heads", None, "side"),
        ),
        out_specs=(
            P("dp", ("heads", "side"), None, None),
            P("dp", None, ("heads", "side")),
            P("dp", None, ("heads", "side")),
        ),
        check_vma=False,
    )
```

```python
import functools

import jax
import jax.numpy as jnp
from jax import lax
from jax.experimental import pallas as pl
from jax.experimental.pallas import tpu as pltpu
from jax.sharding import PartitionSpec as P

F32 = jnp.float32
BF16 = jnp.bfloat16
MESH = pl.DeviceIdType.MESH
SLOTS = 8
LANES = 128
IN_NAMES = ("q", "k", "v", "hg", "res", "ng", "ids", "gates", "state", "wo", "wg", "wu", "wd")


def dot(a, b):
    return jnp.dot(a, b, preferred_element_type=F32)


def kernel(dims, *refs):
    (experts, depth, chunks, rows_y, requests, steps, top, piece, hidden, width) = dims
    tokens = requests * steps
    span = depth // chunks
    wide = span * piece
    lane_groups = wide // LANES
    row_tiles = tokens // 8
    tiles = lane_groups * row_tiles
    per = -(-tiles // span)
    feats = depth * piece
    main = experts * SLOTS
    slots = main + experts
    n_in = len(IN_NAMES)
    hbm = dict(zip(IN_NAMES, refs[:n_in]))
    slope_ref, state_out, resid_out, moe_out = refs[n_in : n_in + 4]
    vm = dict(zip(IN_NAMES, refs[n_in + 4 : 2 * n_in + 4]))
    (
        wdd, ex_src, ex_dst, part, tsum, rs_buf, disp, recv, gain_v,
        ss_src, ss_dst, gu_src, gu_dst, back, comb, rs2_src, rs2_buf,
        in_sem, side_send, side_recv, z_send, z_recv, dp_send, dp_recv,
    ) = refs[2 * n_in + 4 :]

    my_dp = lax.axis_index("dp")
    my_z = lax.axis_index("heads")
    my_side = lax.axis_index("side")
    partner = (my_dp, my_z, 1 - my_side)
    my_chunk = my_z // span
    ahead = [(chunks // 2 + (p + 1) // 2 * (1 - 2 * (p % 2)) + chunks) % chunks for p in range(chunks)]
    order = [(my_chunk + shift) % chunks for shift in ahead]

    def z_peer(i):
        d = depth // 2 - (i + 1) // 2
        sign = 1 - 2 * ((i + 1) % 2)
        return (my_z + sign * d + depth) % depth

    columns = experts // rows_y

    def dp_peer(i):
        x = (my_dp // rows_y + i // rows_y) % columns
        y = (my_dp % rows_y + i % rows_y) % rows_y
        return x * rows_y + y

    def home(i):
        x = (my_dp // rows_y - i // rows_y + columns) % columns
        y = (my_dp % rows_y - i % rows_y + rows_y) % rows_y
        return x * rows_y + y

    def loads(name):
        i = IN_NAMES.index(name)
        return pltpu.make_async_copy(hbm[name], vm[name], in_sem.at[i])

    def to_partner(src, dst, i):
        return pltpu.make_async_remote_copy(
            src_ref=src, dst_ref=dst, send_sem=side_send.at[i], recv_sem=side_recv.at[i],
            device_id=partner, device_id_type=MESH,
        )

    def z_copy(phase, src, dst, peer):
        return pltpu.make_async_remote_copy(
            src_ref=src, dst_ref=dst, send_sem=z_send.at[phase], recv_sem=z_recv.at[phase],
            device_id=(my_dp, peer, my_side), device_id_type=MESH,
        )

    def dp_copy(phase, src, dst, peer):
        return pltpu.make_async_remote_copy(
            src_ref=src, dst_ref=dst, send_sem=dp_send.at[phase], recv_sem=dp_recv.at[phase],
            device_id=(peer, my_z, my_side), device_id_type=MESH,
        )

    for name in ("state", "q", "k", "v", "hg", "wo", "wd", "res", "ids", "gates", "ng", "wg", "wu"):
        loads(name).start()

    barrier = pltpu.get_barrier_semaphore()

    def greet_z(i, c):
        pl.semaphore_signal(barrier, 1, device_id=(my_dp, z_peer(i), my_side), device_id_type=MESH)
        return c

    def greet_dp(i, c):
        pl.semaphore_signal(barrier, 1, device_id=(dp_peer(i), my_z, my_side), device_id_type=MESH)
        return c

    lax.fori_loop(0, depth - 1, greet_z, 0)
    lax.fori_loop(1, experts, greet_dp, 0)
    pl.semaphore_signal(barrier, 1, device_id=partner, device_id_type=MESH)

    for name in ("q", "k", "v", "hg", "state"):
        loads(name).wait()
    decay = jnp.exp(jnp.full((1, LANES), -slope_ref[0], F32))
    q = vm["q"][...].astype(F32)
    k = vm["k"][...].astype(F32)
    v = vm["v"][...].astype(F32)
    q1, q2 = q[:, 0, :], q[:, 1, :]
    k1, k2 = k[:, 0, :], k[:, 1, :]
    v1, v2 = v[:, 0, :], v[:, 1, :]
    read = jnp.einsum(
        "rsi,rij->rsj", vm["q"][...], vm["state"][...].reshape(requests, LANES, LANES),
        preferred_element_type=F32,
    )
    dotted = lambda a, b: jnp.sum(a * b, 1, keepdims=True)
    o1 = decay * read[:, 0, :] + dotted(q1, k1) * v1
    o2 = decay * decay * read[:, 1, :] + decay * (dotted(q2, k1) * v1) + dotted(q2, k2) * v2
    out = jnp.concatenate([o1, o2], 0)
    normed = out * lax.rsqrt(jnp.mean(out * out, 1, keepdims=True) + 1e-6) * vm["hg"][...]
    loads("wo").wait()
    projected = dot(normed.astype(BF16), vm["wo"][...])
    halves = [
        jnp.concatenate(
            [projected[:, (2 * a + s) * piece : (2 * a + s + 1) * piece] for a in range(depth)], 1
        )
        for s in range(2)
    ]
    first = my_side == 0
    ex_src[...] = jnp.where(first, halves[1], halves[0]).astype(BF16)
    own = jnp.where(first, halves[0], halves[1])

    loads("res").wait()
    res = vm["res"][...].astype(F32)
    res = jnp.concatenate([res[:, s, :] for s in range(steps)], 0).astype(BF16)

    def placed(size, at):
        column = lax.broadcasted_iota(jnp.int32, (piece, size), 1)
        row = lax.broadcasted_iota(jnp.int32, (piece, size), 0)
        return (column == row + at * piece).astype(BF16)

    own = own + dot(res, placed(feats, my_z))

    loads("wd").wait()
    for a in range(depth):
        at = a % span * piece
        wdd[a // span, :, at : at + piece] = vm["wd"][:, a, :]

    pl.semaphore_wait(barrier, depth + experts - 1)
    exchange = to_partner(ex_src, ex_dst, 0)
    exchange.start()

    loads("ids").wait()
    loads("gates").wait()
    row_e = lax.broadcasted_iota(jnp.int32, (experts, requests), 0).astype(F32)
    row_m = lax.broadcasted_iota(jnp.int32, (main, requests), 0).astype(F32)
    upper = (
        lax.broadcasted_iota(jnp.int32, (requests, requests), 0)
        < lax.broadcasted_iota(jnp.int32, (requests, requests), 1)
    ).astype(BF16)
    taken = jnp.zeros((experts, 1), F32)
    kinds = 1 + lane_groups
    picks = [[] for _ in range(kinds)]
    shares = [[] for _ in range(kinds)]
    for s in range(steps):
        pick = [jnp.zeros((main, requests), F32) for _ in range(kinds)]
        share = list(pick)
        for c in range(top):
            ids = vm["ids"][s, c : c + 1, :].astype(F32)
            gate = vm["gates"][s, c : c + 1, :]
            onehot = (row_e == ids).astype(F32)
            before = dot(onehot.astype(BF16), upper) + taken
            slot = jnp.sum(onehot * before, 0, keepdims=True)
            taken = taken + jnp.sum(onehot, 1, keepdims=True)
            low = slot < SLOTS
            goals = [jnp.where(low, ids * SLOTS + slot, -1.0)]
            goals += [jnp.where(low, -1.0, ids * SLOTS + j) for j in range(lane_groups)]
            for n, goal in enumerate(goals):
                hit = (row_m == goal).astype(F32)
                pick[n] = pick[n] + hit
                share[n] = share[n] + hit * gate
        for n in range(kinds):
            picks[n].append(pick[n])
            shares[n].append(share[n])
    picks = [jnp.concatenate(p, 1).astype(BF16) for p in picks]

    def split(x):
        high = x.astype(BF16)
        return jnp.concatenate([high, (x - high.astype(F32)).astype(BF16)], 1)

    shares = [split(jnp.concatenate(s, 1).T) for s in shares]
    loads("ng").wait()
    for a in range(depth):
        at = a % span * piece
        gain_v[a // span, :, at : at + piece] = jnp.where(
            first,
            vm["ng"][:, 2 * a * piece : (2 * a + 1) * piece],
            vm["ng"][:, (2 * a + 1) * piece : (2 * a + 2) * piece],
        )
    exchange.wait()
    chip = own + ex_dst[...].astype(F32)
    for c in range(chunks):
        base = c * span * per
        for j in range(lane_groups):
            at = c * wide + j * LANES
            block = chip[:, at : at + LANES].reshape(row_tiles, 8, LANES)
            part[base + j * row_tiles : base + (j + 1) * row_tiles] = block.astype(BF16)
        if span * per > tiles:
            part[base + tiles : base + span * per] = jnp.zeros((span * per - tiles, 8, LANES), BF16)

    def rs_start(i, c):
        peer = z_peer(i)
        z_copy(0, part.at[pl.ds(peer * per, per)], rs_buf.at[i], peer).start()
        return c

    lax.fori_loop(0, depth - 1, rs_start, 0)

    kd = decay * k1
    kd_hi = kd.astype(BF16).astype(F32)
    lhs = jnp.stack([kd_hi, kd - kd_hi, k2], 1).astype(BF16)
    rhs = jnp.stack([v1, v1, v2], 1).astype(BF16)
    decay2 = decay * decay
    for r in range(requests):
        outer = lax.dot_general(
            lhs[r], rhs[r], (((0,), (0,)), ((), ())), preferred_element_type=F32
        )
        state_out[r, 0] = (decay2 * vm["state"][r, 0].astype(F32) + outer).astype(BF16)

    z_copy(0, rs_buf, rs_buf, z_peer(0)).wait()
    mine = pl.ds(my_z * per, per)
    total = part[mine].astype(F32)
    for i in range(depth - 1):
        total = total + rs_buf[i].astype(F32)
    tsum[mine] = total.astype(BF16)

    def ag_start(i, c):
        peer = z_peer(i)
        pltpu.make_async_remote_copy(
            src_ref=tsum.at[mine], dst_ref=tsum.at[mine], send_sem=z_send.at[1],
            recv_sem=z_recv.at[3 + my_chunk], device_id=(my_dp, peer, my_side), device_id_type=MESH,
        ).start()
        return c

    lax.fori_loop(0, depth - 1, ag_start, 0)

    for p, chunk in enumerate(order):
        count = span * per if ahead[p] else (span - 1) * per
        held = tsum.at[pl.ds(0, count)]
        if count:
            pltpu.make_async_remote_copy(
                src_ref=held, dst_ref=held, send_sem=z_send.at[1], recv_sem=z_recv.at[3 + chunk],
                device_id=partner, device_id_type=MESH,
            ).wait_recv()
        cols = []
        for j in range(lane_groups):
            block = tsum[pl.ds(chunk * span * per + j * row_tiles, row_tiles)].astype(F32)
            cols.append(block.reshape(tokens, LANES).astype(BF16))
        last = jnp.zeros((main, LANES), F32)
        for j, col in enumerate(cols):
            disp[p, :, j] = dot(picks[0], col).reshape(experts, SLOTS, LANES).astype(BF16)
            last = last + dot(picks[1 + j], col)
        disp[p, :, lane_groups] = last.reshape(experts, SLOTS, LANES).astype(BF16)

        def go_start(i, c, p=p):
            peer = dp_peer(i)
            dp_copy(p, disp.at[p, peer], recv.at[p, i], peer).start()
            return c

        lax.fori_loop(1, experts, go_start, 0)
        recv[p, 0] = disp[p, my_dp]
        if not ahead[p]:
            resid_out[...] = lax.dot_general(
                jnp.concatenate(cols, 1), placed(wide, my_z % span),
                (((1,), (1,)), ((), ())), preferred_element_type=F32,
            ).astype(BF16)

    z_copy(1, rs_buf, rs_buf, z_peer(0)).wait_send()
    loads("wg").wait()
    loads("wu").wait()
    unpick = [
        (
            lax.broadcasted_iota(jnp.int32, (experts, main), 1)
            == lax.broadcasted_iota(jnp.int32, (experts, main), 0) * SLOTS + j
        ).astype(BF16)
        for j in range(lane_groups)
    ]
    others = pl.ds(1, experts - 1)
    gate_own = jnp.zeros((slots, hidden), F32)
    up_own = jnp.zeros((slots, hidden), F32)
    squares = jnp.zeros((slots, LANES), F32)
    for p, chunk in enumerate(order):
        dp_copy(p, disp.at[p, others], recv.at[p, others], dp_peer(1)).wait()
        last = recv[p, :, lane_groups].astype(F32).reshape(main, LANES).astype(BF16)
        xs = []
        for j in range(lane_groups):
            x = jnp.concatenate(
                [recv[p, :, j].astype(F32).reshape(main, LANES), dot(unpick[j], last)], 0
            )
            squares = squares + x * x
            xs.append((x * gain_v[chunk][:, j * LANES : (j + 1) * LANES]).astype(BF16))
        x = jnp.concatenate(xs, 1)
        rows = pl.ds(chunk * span, span)
        gate_own = gate_own + dot(x, vm["wg"][rows].reshape(wide, hidden))
        up_own = up_own + dot(x, vm["wu"][rows].reshape(wide, hidden))
    gu_src[0] = gate_own.astype(BF16)
    gu_src[1] = up_own.astype(BF16)
    ss_src[...] = jnp.broadcast_to(jnp.sum(squares, 1, keepdims=True), (slots, LANES))
    gu_copy = to_partner(gu_src, gu_dst, 1)
    ss_copy = to_partner(ss_src, ss_dst, 2)
    gu_copy.start()
    ss_copy.start()
    ss_copy.wait()
    scale = lax.rsqrt((ss_src[...] + ss_dst[...]) / width + 1e-6)[:, :1]
    gu_copy.wait()
    gate_val = (gate_own + gu_dst[0].astype(F32)) * scale
    up_val = (up_own + gu_dst[1].astype(F32)) * scale
    act = (gate_val / (1.0 + jnp.exp(-gate_val)) * up_val).astype(BF16)

    for p, chunk in enumerate(order):
        down = dot(act, wdd[chunk])
        last = jnp.zeros((main, LANES), F32)
        for j in range(lane_groups):
            col = down[:, j * LANES : (j + 1) * LANES]
            back[p, :, j] = col[:main].reshape(experts, SLOTS, LANES).astype(BF16)
            last = last + lax.dot_general(
                unpick[j], col[main:].astype(BF16), (((0,), (0,)), ((), ())),
                preferred_element_type=F32,
            )
        back[p, :, lane_groups] = last.reshape(experts, SLOTS, LANES).astype(BF16)

        def back_start(i, c, p=p):
            dp_copy(chunks + p, back.at[p, i], comb.at[p, my_dp], home(i)).start()
            return c

        lax.fori_loop(1, experts, back_start, 0)
        comb[p, my_dp] = back[p, 0]

    for p, chunk in enumerate(order):
        dp_copy(chunks + p, back.at[p, others], comb.at[p, others], dp_peer(1)).wait()
        last = comb[p, :, lane_groups].astype(F32).reshape(main, LANES).astype(BF16)
        twice = jnp.concatenate([last, last], 0)
        cols = []
        for j in range(lane_groups):
            got = comb[p, :, j].astype(F32).reshape(main, LANES).astype(BF16)
            got = jnp.concatenate([got, got], 0)
            cols.append(dot(shares[0], got) + dot(shares[1 + j], twice))
        mixed = jnp.concatenate(cols, 1)
        for b in range(span):
            lanes = [
                mixed[t * 8 : t * 8 + 8, b * piece : (b + 1) * piece] for t in range(row_tiles)
            ]
            pad = rs2_buf.shape[2] - row_tiles * piece
            if pad:
                lanes.append(jnp.zeros((8, pad), F32))
            rs2_src[p, b] = jnp.concatenate(lanes, 1).astype(BF16)
        for b in range(span):
            peer = chunk * span + b

            def send(p=p, b=b, peer=peer):
                z_copy(2, rs2_src.at[p, b], rs2_buf.at[my_z], peer).start()

            if ahead[p]:
                send()
            else:
                pl.when(peer != my_z)(send)
    rs2_buf[my_z] = rs2_src[chunks - 1, my_z % span]
    arrived = rs2_buf.at[pl.ds(0, depth - 1)]
    z_copy(2, arrived, arrived, z_peer(0)).wait()
    final = rs2_buf[0].astype(F32)
    for i in range(1, depth):
        final = final + rs2_buf[i].astype(F32)
    for t in range(row_tiles):
        moe_out[t * 8 : t * 8 + 8, :] = final[:, t * piece : (t + 1) * piece].astype(BF16)


def layer(mesh_shape, q, k, v, state, slopes, hg, wo, res, ng, ids, gates, wg, wu, wd):
    experts, depth = mesh_shape["dp"], mesh_shape["heads"]
    requests, steps, head = q.shape
    piece = res.shape[2]
    hidden = wg.shape[3]
    top = ids.shape[2]
    width = ng.shape[0]
    tokens = requests * steps
    feats = depth * piece
    chunks = max(1, depth // 4)
    span = depth // chunks
    wide = span * piece
    per = -(-(wide // LANES) * (tokens // 8) // span)
    slots = experts * SLOTS + experts
    packed = -(-(tokens // 8) * piece // LANES) * LANES
    tiled = (chunks, experts, wide // LANES + 1, SLOTS, LANES)
    rows_y = 4 if experts == 16 else experts
    dims = (experts, depth, chunks, rows_y, requests, steps, top, piece, hidden, width)
    operands = {
        "q": q, "k": k, "v": v, "hg": hg.reshape(1, head), "res": res, "ng": ng.reshape(1, width),
        "ids": ids.transpose(1, 2, 0), "gates": gates.transpose(1, 2, 0), "state": state, "wo": wo,
        "wg": wg[0], "wu": wu[0], "wd": wd[0],
    }
    arrays = [operands[name] for name in IN_NAMES]
    dma = pltpu.SemaphoreType.DMA
    scratch = [pltpu.VMEM(a.shape, a.dtype) for a in arrays] + [
        pltpu.VMEM((chunks, hidden, wide), BF16),
        pltpu.VMEM((tokens, feats), BF16),
        pltpu.VMEM((tokens, feats), BF16),
        pltpu.VMEM((per * depth, 8, LANES), BF16),
        pltpu.VMEM((per * depth, 8, LANES), BF16),
        pltpu.VMEM((depth - 1, per, 8, LANES), BF16),
        pltpu.VMEM(tiled, BF16),
        pltpu.VMEM(tiled, BF16),
        pltpu.VMEM((chunks, 1, wide), F32),
        pltpu.VMEM((slots, LANES), F32),
        pltpu.VMEM((slots, LANES), F32),
        pltpu.VMEM((2, slots, hidden), BF16),
        pltpu.VMEM((2, slots, hidden), BF16),
        pltpu.VMEM(tiled, BF16),
        pltpu.VMEM(tiled, BF16),
        pltpu.VMEM((chunks, span, 8, packed), BF16),
        pltpu.VMEM((depth, 8, packed), BF16),
        dma((len(IN_NAMES),)),
        dma((3,)),
        dma((3,)),
        dma((3,)),
        dma((3 + chunks,)),
        dma((2 * chunks,)),
        dma((2 * chunks,)),
    ]
    any_spec = pl.BlockSpec(memory_space=pl.ANY)
    state_new, resid, moe = pl.pallas_call(
        functools.partial(kernel, dims),
        out_shape=(
            pltpu.VMEM(state.shape, BF16),
            pltpu.VMEM((tokens, piece), BF16),
            pltpu.VMEM((tokens, piece), BF16),
        ),
        in_specs=[any_spec] * len(arrays) + [pl.BlockSpec(memory_space=pltpu.SMEM)],
        out_specs=(
            pl.BlockSpec(memory_space=pltpu.VMEM),
            pl.BlockSpec(memory_space=pltpu.VMEM),
            pl.BlockSpec(memory_space=pltpu.VMEM),
        ),
        scratch_shapes=scratch,
        compiler_params=pltpu.CompilerParams(
            collective_id=0, has_side_effects=True, vmem_limit_bytes=56 * 1024 * 1024
        ),
        name="layer",
    )(*arrays, slopes)
    back = lambda x: x.reshape(steps, requests, piece).transpose(1, 0, 2)
    return state_new, back(resid), back(moe)


def solution(mesh):
    return jax.shard_map(
        functools.partial(layer, dict(mesh.shape)),
        mesh=mesh,
        in_specs=(
            P("dp", None, ("heads", "side")),
            P("dp", None, ("heads", "side")),
            P("dp", None, ("heads", "side")),
            P("dp", ("heads", "side"), None, None),
            P(("heads", "side")),
            P(("heads", "side")),
            P(("heads", "side"), None),
            P("dp", None, ("heads", "side")),
            P(),
            P("dp", None, None),
            P("dp", None, None),
            P("dp", None, "side", "heads"),
            P("dp", None, "side", "heads"),
            P("dp", "heads", None, "side"),
        ),
        out_specs=(
            P("dp", ("heads", "side"), None, None),
            P("dp", None, ("heads", "side")),
            P("dp", None, ("heads", "side")),
        ),
        check_vma=False,
    )
```

```python
import functools

import jax
import jax.numpy as jnp
from jax import lax
from jax.experimental import pallas as pl
from jax.experimental.pallas import tpu as pltpu
from jax.sharding import PartitionSpec as P

F32 = jnp.float32
BF16 = jnp.bfloat16
MESH = pl.DeviceIdType.MESH
SLOTS = 8
LANES = 128
IN_NAMES = ("q", "k", "v", "hg", "res", "ng", "ids", "gates", "state", "wo", "wg", "wu", "wd")


def dot(a, b):
    return jnp.dot(a, b, preferred_element_type=F32)


def kernel(dims, *refs):
    (experts, depth, chunks, rows_y, requests, steps, top, piece, hidden, width) = dims
    tokens = requests * steps
    span = depth // chunks
    wide = span * piece
    lane_groups = wide // LANES
    row_tiles = tokens // 8
    tiles = lane_groups * row_tiles
    per = -(-tiles // span)
    feats = depth * piece
    main = experts * SLOTS
    slots = main + experts
    n_in = len(IN_NAMES)
    hbm = dict(zip(IN_NAMES, refs[:n_in]))
    slope_ref, state_out, resid_out, moe_out = refs[n_in : n_in + 4]
    vm = dict(zip(IN_NAMES, refs[n_in + 4 : 2 * n_in + 4]))
    (
        wdd, ex_src, ex_dst, part, tsum, inbox, relay, disp, recv, gain_v,
        ss_src, ss_dst, gu_src, gu_dst, back, comb, part2, inbox2, relay2,
        in_sem, side_send, side_recv, z_send, z_recv, dp_send, dp_recv,
    ) = refs[2 * n_in + 4 :]

    my_dp = lax.axis_index("dp")
    my_z = lax.axis_index("heads")
    my_side = lax.axis_index("side")
    partner = (my_dp, my_z, 1 - my_side)
    my_chunk = my_z // span
    ahead = [(chunks // 2 + (p + 1) // 2 * (1 - 2 * (p % 2)) + chunks) % chunks for p in range(chunks)]
    order = [(my_chunk + shift) % chunks for shift in ahead]
    nearest = sorted(range(chunks), key=lambda shift: min(shift, chunks - shift))
    near_order = [(my_chunk + shift) % chunks for shift in nearest]
    hop = depth // 4

    def z_at(offset):
        return (my_z + offset + depth) % depth

    columns = experts // rows_y

    def dp_peer(i):
        x = (my_dp // rows_y + i // rows_y) % columns
        y = (my_dp % rows_y + i % rows_y) % rows_y
        return x * rows_y + y

    def home(i):
        x = (my_dp // rows_y - i // rows_y + columns) % columns
        y = (my_dp % rows_y - i % rows_y + rows_y) % rows_y
        return x * rows_y + y

    def loads(name):
        i = IN_NAMES.index(name)
        return pltpu.make_async_copy(hbm[name], vm[name], in_sem.at[i])

    def to_partner(src, dst, i):
        return pltpu.make_async_remote_copy(
            src_ref=src, dst_ref=dst, send_sem=side_send.at[i], recv_sem=side_recv.at[i],
            device_id=partner, device_id_type=MESH,
        )

    def dp_copy(phase, src, dst, peer):
        return pltpu.make_async_remote_copy(
            src_ref=src, dst_ref=dst, send_sem=dp_send.at[phase], recv_sem=dp_recv.at[phase],
            device_id=(peer, my_z, my_side), device_id_type=MESH,
        )

    for name in ("state", "q", "k", "v", "hg", "wo", "wd", "res", "ids", "gates", "ng", "wg", "wu"):
        loads(name).start()

    barrier = pltpu.get_barrier_semaphore()

    def greet_dp(i, c):
        pl.semaphore_signal(barrier, 1, device_id=(dp_peer(i), my_z, my_side), device_id_type=MESH)
        return c

    for offset in range(hop, 0, -1):
        for sign in (1, -1):
            pl.semaphore_signal(
                barrier, 1, device_id=(my_dp, z_at(sign * offset), my_side), device_id_type=MESH
            )
    lax.fori_loop(1, experts, greet_dp, 0)
    pl.semaphore_signal(barrier, 1, device_id=partner, device_id_type=MESH)

    for name in ("q", "k", "v", "hg", "state"):
        loads(name).wait()
    decay = jnp.exp(jnp.full((1, LANES), -slope_ref[0], F32))
    q = vm["q"][...].astype(F32)
    k = vm["k"][...].astype(F32)
    v = vm["v"][...].astype(F32)
    q1, q2 = q[:, 0, :], q[:, 1, :]
    k1, k2 = k[:, 0, :], k[:, 1, :]
    v1, v2 = v[:, 0, :], v[:, 1, :]
    read = jnp.einsum(
        "rsi,rij->rsj", vm["q"][...], vm["state"][...].reshape(requests, LANES, LANES),
        preferred_element_type=F32,
    )
    dotted = lambda a, b: jnp.sum(a * b, 1, keepdims=True)
    o1 = decay * read[:, 0, :] + dotted(q1, k1) * v1
    o2 = decay * decay * read[:, 1, :] + decay * (dotted(q2, k1) * v1) + dotted(q2, k2) * v2
    out = jnp.concatenate([o1, o2], 0)
    normed = out * lax.rsqrt(jnp.mean(out * out, 1, keepdims=True) + 1e-6) * vm["hg"][...]
    loads("wo").wait()
    projected = dot(normed.astype(BF16), vm["wo"][...])
    halves = [
        jnp.concatenate(
            [projected[:, (2 * a + s) * piece : (2 * a + s + 1) * piece] for a in range(depth)], 1
        )
        for s in range(2)
    ]
    first = my_side == 0
    ex_src[...] = jnp.where(first, halves[1], halves[0]).astype(BF16)
    own = jnp.where(first, halves[0], halves[1])

    loads("res").wait()
    res = vm["res"][...].astype(F32)
    res = jnp.concatenate([res[:, s, :] for s in range(steps)], 0).astype(BF16)

    def placed(size, at):
        column = lax.broadcasted_iota(jnp.int32, (piece, size), 1)
        row = lax.broadcasted_iota(jnp.int32, (piece, size), 0)
        return (column == row + at * piece).astype(BF16)

    own = own + dot(res, placed(feats, my_z))

    pl.semaphore_wait(barrier, 2 * hop + experts)
    exchange = to_partner(ex_src, ex_dst, 0)
    exchange.start()

    loads("ids").wait()
    loads("gates").wait()
    row_e = lax.broadcasted_iota(jnp.int32, (experts, requests), 0).astype(F32)
    row_m = lax.broadcasted_iota(jnp.int32, (main, requests), 0).astype(F32)
    upper = (
        lax.broadcasted_iota(jnp.int32, (requests, requests), 0)
        < lax.broadcasted_iota(jnp.int32, (requests, requests), 1)
    ).astype(BF16)
    taken = jnp.zeros((experts, 1), F32)
    kinds = 1 + lane_groups
    picks = [[] for _ in range(kinds)]
    shares = [[] for _ in range(kinds)]
    for s in range(steps):
        pick = [jnp.zeros((main, requests), F32) for _ in range(kinds)]
        share = list(pick)
        for c in range(top):
            ids = vm["ids"][s, c : c + 1, :].astype(F32)
            gate = vm["gates"][s, c : c + 1, :]
            onehot = (row_e == ids).astype(F32)
            before = dot(onehot.astype(BF16), upper) + taken
            slot = jnp.sum(onehot * before, 0, keepdims=True)
            taken = taken + jnp.sum(onehot, 1, keepdims=True)
            low = slot < SLOTS
            goals = [jnp.where(low, ids * SLOTS + slot, -1.0)]
            goals += [jnp.where(low, -1.0, ids * SLOTS + j) for j in range(lane_groups)]
            for n, goal in enumerate(goals):
                hit = (row_m == goal).astype(F32)
                pick[n] = pick[n] + hit
                share[n] = share[n] + hit * gate
        for n in range(kinds):
            picks[n].append(pick[n])
            shares[n].append(share[n])
    picks = [jnp.concatenate(p, 1).astype(BF16) for p in picks]

    def split(x):
        high = x.astype(BF16)
        return jnp.concatenate([high, (x - high.astype(F32)).astype(BF16)], 1)

    shares = [split(jnp.concatenate(s, 1).T) for s in shares]
    loads("ng").wait()
    for a in range(depth):
        at = a % span * piece
        gain_v[a // span, :, at : at + piece] = jnp.where(
            first,
            vm["ng"][:, 2 * a * piece : (2 * a + 1) * piece],
            vm["ng"][:, (2 * a + 1) * piece : (2 * a + 2) * piece],
        )
    exchange.wait()
    chip = own + ex_dst[...].astype(F32)
    for c in range(chunks):
        base = c * span * per
        for j in range(lane_groups):
            at = c * wide + j * LANES
            rows = chip[:, at : at + LANES].reshape(row_tiles, 8, LANES)
            part[base + j * row_tiles : base + (j + 1) * row_tiles] = rows.astype(BF16)
        if span * per > tiles:
            part[base + tiles : base + span * per] = jnp.zeros((span * per - tiles, 8, LANES), BF16)

    direct = 2 * hop - 1

    def block(ref, z):
        return ref.at[pl.ds(z * per, per)]

    def rs_send(src, box, base, down):
        up = depth - down
        below = down <= 2 * hop
        near = jnp.where(below, down < hop, up < hop)
        step = jnp.where(below, -jnp.where(near, down, down - hop), jnp.where(near, up, up - hop))
        length = jnp.abs(step) - 1
        slot = jnp.where(
            near,
            direct + length + jnp.where(below, 0, hop - 1),
            length + jnp.where(below, 0, hop),
        )
        group = base + jnp.where(near, 2, jnp.where(below, 0, 1))
        pltpu.make_async_remote_copy(
            src_ref=block(src, z_at(-down)), dst_ref=box.at[slot], send_sem=z_send.at[base],
            recv_sem=z_recv.at[group], device_id=(my_dp, z_at(step), my_side), device_id_type=MESH,
        ).start()

    def rs_relay(src, box, out, base, side):
        first_slot, count = ((0, hop), (hop, hop - 1))[side]
        sign = (-1, 1)[side]
        held = box.at[pl.ds(first_slot, count)]
        z_wait(held, base + side).wait_recv()
        total = src[pl.ds(z_at(sign * hop) * per, per)].astype(F32)
        for n in range(count):
            total = total + box[first_slot + n].astype(F32)
        out[side] = total.astype(BF16)
        pltpu.make_async_remote_copy(
            src_ref=out.at[side], dst_ref=box.at[depth - 3 + side], send_sem=z_send.at[base],
            recv_sem=z_recv.at[base + 2], device_id=(my_dp, z_at(sign * hop), my_side),
            device_id_type=MESH,
        ).start()

    def z_wait(held, group, send=0):
        return pltpu.make_async_remote_copy(
            src_ref=held, dst_ref=held, send_sem=z_send.at[send], recv_sem=z_recv.at[group],
            device_id=partner, device_id_type=MESH,
        )

    def rs_total(src, box, base):
        z_wait(box.at[pl.ds(direct, 2 * hop)], base + 2).wait_recv()
        total = src[pl.ds(my_z * per, per)].astype(F32)
        for n in range(direct, depth - 1):
            total = total + box[n].astype(F32)
        z_wait(box, base, base).wait_send()
        return total

    downs = [n for d in range(hop, 0, -1) for n in (hop + d, depth - hop - d)]
    downs += [n for d in range(hop - 1, 0, -1) for n in (d, depth - d)]
    for down in dict.fromkeys(downs):
        rs_send(part, inbox, 0, jnp.int32(down))

    loads("wd").wait()
    for a in range(depth):
        at = a % span * piece
        wdd[a // span, :, at : at + piece] = vm["wd"][:, a, :]

    rs_relay(part, inbox, relay, 0, 0)
    rs_relay(part, inbox, relay, 0, 1)

    kd = decay * k1
    kd_hi = kd.astype(BF16).astype(F32)
    lhs = jnp.stack([kd_hi, kd - kd_hi, k2], 1).astype(BF16)
    rhs = jnp.stack([v1, v1, v2], 1).astype(BF16)
    decay2 = decay * decay
    for r in range(requests):
        outer = lax.dot_general(
            lhs[r], rhs[r], (((0,), (0,)), ((), ())), preferred_element_type=F32
        )
        state_out[r, 0] = (decay2 * vm["state"][r, 0].astype(F32) + outer).astype(BF16)

    mine = pl.ds(my_z * per, per)
    tsum[mine] = rs_total(part, inbox, 0).astype(BF16)

    def ag_copy(origin, to):
        held = block(tsum, origin)
        return pltpu.make_async_remote_copy(
            src_ref=held, dst_ref=held, send_sem=z_send.at[1], recv_sem=z_recv.at[6 + origin],
            device_id=(my_dp, to, my_side), device_id_type=MESH,
        )

    for offset in range(hop, 0, -1):
        for sign in (1, -1):
            ag_copy(my_z, z_at(sign * offset)).start()
    for sign, reach in ((1, hop), (-1, hop - 1)):
        origin = z_at(-sign * hop)
        ag_copy(origin, z_at(sign)).wait_recv()
        for offset in range(reach, 0, -1):
            ag_copy(origin, z_at(sign * offset)).start()

    for p, chunk in enumerate(near_order):
        for b in range(span):
            origin = chunk * span + b
            away = (origin - my_z + depth) % depth

            def arrive(origin=origin):
                ag_copy(origin, z_at(1)).wait_recv()

            pl.when((away != 0) & (away != hop) & (away != depth - hop))(arrive)
        cols = []
        for j in range(lane_groups):
            rows = tsum[pl.ds(chunk * span * per + j * row_tiles, row_tiles)].astype(F32)
            cols.append(rows.reshape(tokens, LANES).astype(BF16))
        last = jnp.zeros((main, LANES), F32)
        for j, col in enumerate(cols):
            disp[p, :, j] = dot(picks[0], col).reshape(experts, SLOTS, LANES).astype(BF16)
            last = last + dot(picks[1 + j], col)
        disp[p, :, lane_groups] = last.reshape(experts, SLOTS, LANES).astype(BF16)

        def go_start(i, c, p=p):
            peer = dp_peer(i)
            dp_copy(p, disp.at[p, peer], recv.at[p, i], peer).start()
            return c

        lax.fori_loop(1, experts, go_start, 0)
        recv[p, 0] = disp[p, my_dp]
        if not nearest[p]:
            resid_out[...] = lax.dot_general(
                jnp.concatenate(cols, 1), placed(wide, my_z % span),
                (((1,), (1,)), ((), ())), preferred_element_type=F32,
            ).astype(BF16)

    z_wait(inbox, 6, 1).wait_send()
    loads("wg").wait()
    loads("wu").wait()
    unpick = [
        (
            lax.broadcasted_iota(jnp.int32, (experts, main), 1)
            == lax.broadcasted_iota(jnp.int32, (experts, main), 0) * SLOTS + j
        ).astype(BF16)
        for j in range(lane_groups)
    ]
    others = pl.ds(1, experts - 1)
    gate_own = jnp.zeros((slots, hidden), F32)
    up_own = jnp.zeros((slots, hidden), F32)
    squares = jnp.zeros((slots, LANES), F32)
    for p, chunk in enumerate(near_order):
        dp_copy(p, disp.at[p, others], recv.at[p, others], dp_peer(1)).wait()
        last = recv[p, :, lane_groups].astype(F32).reshape(main, LANES).astype(BF16)
        xs = []
        for j in range(lane_groups):
            x = jnp.concatenate(
                [recv[p, :, j].astype(F32).reshape(main, LANES), dot(unpick[j], last)], 0
            )
            squares = squares + x * x
            xs.append((x * gain_v[chunk][:, j * LANES : (j + 1) * LANES]).astype(BF16))
        x = jnp.concatenate(xs, 1)
        rows = pl.ds(chunk * span, span)
        gate_own = gate_own + dot(x, vm["wg"][rows].reshape(wide, hidden))
        up_own = up_own + dot(x, vm["wu"][rows].reshape(wide, hidden))
    gu_src[0] = gate_own.astype(BF16)
    gu_src[1] = up_own.astype(BF16)
    ss_src[...] = jnp.broadcast_to(jnp.sum(squares, 1, keepdims=True), (slots, LANES))
    gu_copy = to_partner(gu_src, gu_dst, 1)
    ss_copy = to_partner(ss_src, ss_dst, 2)
    gu_copy.start()
    ss_copy.start()
    ss_copy.wait()
    scale = lax.rsqrt((ss_src[...] + ss_dst[...]) / width + 1e-6)[:, :1]
    gu_copy.wait()
    gate_val = (gate_own + gu_dst[0].astype(F32)) * scale
    up_val = (up_own + gu_dst[1].astype(F32)) * scale
    act = (gate_val / (1.0 + jnp.exp(-gate_val)) * up_val).astype(BF16)

    for p, chunk in enumerate(order):
        down = dot(act, wdd[chunk])
        last = jnp.zeros((main, LANES), F32)
        for j in range(lane_groups):
            col = down[:, j * LANES : (j + 1) * LANES]
            back[p, :, j] = col[:main].reshape(experts, SLOTS, LANES).astype(BF16)
            last = last + lax.dot_general(
                unpick[j], col[main:].astype(BF16), (((0,), (0,)), ((), ())),
                preferred_element_type=F32,
            )
        back[p, :, lane_groups] = last.reshape(experts, SLOTS, LANES).astype(BF16)

        def back_start(i, c, p=p):
            dp_copy(chunks + p, back.at[p, i], comb.at[p, my_dp], home(i)).start()
            return c

        lax.fori_loop(1, experts, back_start, 0)
        comb[p, my_dp] = back[p, 0]

    for p, chunk in enumerate(order):
        dp_copy(chunks + p, back.at[p, others], comb.at[p, others], dp_peer(1)).wait()
        last = comb[p, :, lane_groups].astype(F32).reshape(main, LANES).astype(BF16)
        twice = jnp.concatenate([last, last], 0)
        cols = []
        for j in range(lane_groups):
            got = comb[p, :, j].astype(F32).reshape(main, LANES).astype(BF16)
            got = jnp.concatenate([got, got], 0)
            cols.append(dot(shares[0], got) + dot(shares[1 + j], twice))
        mixed = jnp.concatenate(cols, 1)
        for b in range(span):
            lanes = [
                mixed[t * 8 : t * 8 + 8, b * piece : (b + 1) * piece] for t in range(row_tiles)
            ]
            if per * LANES > row_tiles * piece:
                lanes.append(jnp.zeros((8, per * LANES - row_tiles * piece), F32))
            packed = jnp.concatenate(lanes, 1)
            dest = chunk * span + b
            for t in range(per):
                part2[dest * per + t] = packed[:, t * LANES : (t + 1) * LANES].astype(BF16)
        for b in range(span):
            down = (my_z - chunk * span - b + depth) % depth

            def send(down=down):
                rs_send(part2, inbox2, 3, down)

            pl.when((down != 0) & (down != hop) & (down != depth - hop))(send)
        if hop == span and ahead[p] == 1:
            rs_relay(part2, inbox2, relay2, 3, 1)
        if hop == span and ahead[p] == chunks - 1:
            rs_relay(part2, inbox2, relay2, 3, 0)
    if hop != span:
        rs_relay(part2, inbox2, relay2, 3, 0)
        rs_relay(part2, inbox2, relay2, 3, 1)
    total = rs_total(part2, inbox2, 3)
    final = jnp.concatenate([total[t] for t in range(per)], 1)
    for t in range(row_tiles):
        moe_out[t * 8 : t * 8 + 8, :] = final[:, t * piece : (t + 1) * piece].astype(BF16)


def layer(mesh_shape, q, k, v, state, slopes, hg, wo, res, ng, ids, gates, wg, wu, wd):
    experts, depth = mesh_shape["dp"], mesh_shape["heads"]
    requests, steps, head = q.shape
    piece = res.shape[2]
    hidden = wg.shape[3]
    top = ids.shape[2]
    width = ng.shape[0]
    tokens = requests * steps
    feats = depth * piece
    chunks = max(1, depth // 4)
    span = depth // chunks
    wide = span * piece
    per = -(-(wide // LANES) * (tokens // 8) // span)
    slots = experts * SLOTS + experts
    tiled = (chunks, experts, wide // LANES + 1, SLOTS, LANES)
    rows_y = 4 if experts == 16 else experts
    dims = (experts, depth, chunks, rows_y, requests, steps, top, piece, hidden, width)
    operands = {
        "q": q, "k": k, "v": v, "hg": hg.reshape(1, head), "res": res, "ng": ng.reshape(1, width),
        "ids": ids.transpose(1, 2, 0), "gates": gates.transpose(1, 2, 0), "state": state, "wo": wo,
        "wg": wg[0], "wu": wu[0], "wd": wd[0],
    }
    arrays = [operands[name] for name in IN_NAMES]
    dma = pltpu.SemaphoreType.DMA
    scratch = [pltpu.VMEM(a.shape, a.dtype) for a in arrays] + [
        pltpu.VMEM((chunks, hidden, wide), BF16),
        pltpu.VMEM((tokens, feats), BF16),
        pltpu.VMEM((tokens, feats), BF16),
        pltpu.VMEM((per * depth, 8, LANES), BF16),
        pltpu.VMEM((per * depth, 8, LANES), BF16),
        pltpu.VMEM((depth - 1, per, 8, LANES), BF16),
        pltpu.VMEM((2, per, 8, LANES), BF16),
        pltpu.VMEM(tiled, BF16),
        pltpu.VMEM(tiled, BF16),
        pltpu.VMEM((chunks, 1, wide), F32),
        pltpu.VMEM((slots, LANES), F32),
        pltpu.VMEM((slots, LANES), F32),
        pltpu.VMEM((2, slots, hidden), BF16),
        pltpu.VMEM((2, slots, hidden), BF16),
        pltpu.VMEM(tiled, BF16),
        pltpu.VMEM(tiled, BF16),
        pltpu.VMEM((per * depth, 8, LANES), BF16),
        pltpu.VMEM((depth - 1, per, 8, LANES), BF16),
        pltpu.VMEM((2, per, 8, LANES), BF16),
        dma((len(IN_NAMES),)),
        dma((3,)),
        dma((3,)),
        dma((4,)),
        dma((6 + depth,)),
        dma((2 * chunks,)),
        dma((2 * chunks,)),
    ]
    any_spec = pl.BlockSpec(memory_space=pl.ANY)
    state_new, resid, moe = pl.pallas_call(
        functools.partial(kernel, dims),
        out_shape=(
            pltpu.VMEM(state.shape, BF16),
            pltpu.VMEM((tokens, piece), BF16),
            pltpu.VMEM((tokens, piece), BF16),
        ),
        in_specs=[any_spec] * len(arrays) + [pl.BlockSpec(memory_space=pltpu.SMEM)],
        out_specs=(
            pl.BlockSpec(memory_space=pltpu.VMEM),
            pl.BlockSpec(memory_space=pltpu.VMEM),
            pl.BlockSpec(memory_space=pltpu.VMEM),
        ),
        scratch_shapes=scratch,
        compiler_params=pltpu.CompilerParams(
            collective_id=0, has_side_effects=True, vmem_limit_bytes=56 * 1024 * 1024
        ),
        name="layer",
    )(*arrays, slopes)
    back = lambda x: x.reshape(steps, requests, piece).transpose(1, 0, 2)
    return state_new, back(resid), back(moe)


def solution(mesh):
    return jax.shard_map(
        functools.partial(layer, dict(mesh.shape)),
        mesh=mesh,
        in_specs=(
            P("dp", None, ("heads", "side")),
            P("dp", None, ("heads", "side")),
            P("dp", None, ("heads", "side")),
            P("dp", ("heads", "side"), None, None),
            P(("heads", "side")),
            P(("heads", "side")),
            P(("heads", "side"), None),
            P("dp", None, ("heads", "side")),
            P(),
            P("dp", None, None),
            P("dp", None, None),
            P("dp", None, "side", "heads"),
            P("dp", None, "side", "heads"),
            P("dp", "heads", None, "side"),
        ),
        out_specs=(
            P("dp", ("heads", "side"), None, None),
            P("dp", None, ("heads", "side")),
            P("dp", None, ("heads", "side")),
        ),
        check_vma=False,
    )
```

```python
import functools

import jax
import jax.numpy as jnp
from jax import lax
from jax.experimental import pallas as pl
from jax.experimental.pallas import tpu as pltpu
from jax.sharding import PartitionSpec as P

F32 = jnp.float32
BF16 = jnp.bfloat16
MESH = pl.DeviceIdType.MESH
SLOTS = 8
LANES = 128
IN_NAMES = ("q", "k", "v", "hg", "res", "ng", "ids", "gates", "state", "wo", "wg", "wu", "wd")


def dot(a, b):
    return jnp.dot(a, b, preferred_element_type=F32)


def kernel(dims, *refs):
    (experts, depth, chunks, rows_y, requests, steps, top, piece, hidden, width) = dims
    tokens = requests * steps
    span = depth // chunks
    wide = span * piece
    lane_groups = wide // LANES
    row_tiles = tokens // 8
    tiles = lane_groups * row_tiles
    per = -(-tiles // span)
    feats = depth * piece
    main = experts * SLOTS
    slots = main + experts
    n_in = len(IN_NAMES)
    hbm = dict(zip(IN_NAMES, refs[:n_in]))
    slope_ref, state_out, resid_out, moe_out = refs[n_in : n_in + 4]
    vm = dict(zip(IN_NAMES, refs[n_in + 4 : 2 * n_in + 4]))
    (
        wdd, ex_src, ex_dst, part, tsum, inbox, relay, disp, recv, gain_v,
        ss_src, ss_dst, gu_src, gu_dst, back, comb, part2, inbox2,
        in_sem, side_send, side_recv, z_send, z_recv, dp_send, dp_recv,
    ) = refs[2 * n_in + 4 :]

    my_dp = lax.axis_index("dp")
    my_z = lax.axis_index("heads")
    my_side = lax.axis_index("side")
    partner = (my_dp, my_z, 1 - my_side)
    my_chunk = my_z // span
    ahead = [(chunks // 2 + (p + 1) // 2 * (1 - 2 * (p % 2)) + chunks) % chunks for p in range(chunks)]
    order = [(my_chunk + shift) % chunks for shift in ahead]
    nearest = sorted(range(chunks), key=lambda shift: min(shift, chunks - shift))
    near_order = [(my_chunk + shift) % chunks for shift in nearest]
    hop = depth // 4

    def z_at(offset):
        return (my_z + offset + depth) % depth

    columns = experts // rows_y

    def dp_peer(i):
        x = (my_dp // rows_y + i // rows_y) % columns
        y = (my_dp % rows_y + i % rows_y) % rows_y
        return x * rows_y + y

    def home(i):
        x = (my_dp // rows_y - i // rows_y + columns) % columns
        y = (my_dp % rows_y - i % rows_y + rows_y) % rows_y
        return x * rows_y + y

    def loads(name):
        i = IN_NAMES.index(name)
        return pltpu.make_async_copy(hbm[name], vm[name], in_sem.at[i])

    def to_partner(src, dst, i):
        return pltpu.make_async_remote_copy(
            src_ref=src, dst_ref=dst, send_sem=side_send.at[i], recv_sem=side_recv.at[i],
            device_id=partner, device_id_type=MESH,
        )

    def dp_copy(phase, src, dst, peer):
        return pltpu.make_async_remote_copy(
            src_ref=src, dst_ref=dst, send_sem=dp_send.at[phase], recv_sem=dp_recv.at[phase],
            device_id=(peer, my_z, my_side), device_id_type=MESH,
        )

    for name in ("state", "q", "k", "v", "hg", "wo", "wd", "res", "ids", "gates", "ng", "wg", "wu"):
        loads(name).start()

    barrier = pltpu.get_barrier_semaphore()

    def greet_dp(i, c):
        pl.semaphore_signal(barrier, 1, device_id=(dp_peer(i), my_z, my_side), device_id_type=MESH)
        return c

    for offset in range(hop, 0, -1):
        for sign in (1, -1):
            pl.semaphore_signal(
                barrier, 1, device_id=(my_dp, z_at(sign * offset), my_side), device_id_type=MESH
            )
    lax.fori_loop(1, experts, greet_dp, 0)
    pl.semaphore_signal(barrier, 1, device_id=partner, device_id_type=MESH)

    for name in ("q", "k", "v", "hg", "state"):
        loads(name).wait()
    decay = jnp.exp(jnp.full((1, LANES), -slope_ref[0], F32))
    q = vm["q"][...].astype(F32)
    k = vm["k"][...].astype(F32)
    v = vm["v"][...].astype(F32)
    q1, q2 = q[:, 0, :], q[:, 1, :]
    k1, k2 = k[:, 0, :], k[:, 1, :]
    v1, v2 = v[:, 0, :], v[:, 1, :]
    read = jnp.einsum(
        "rsi,rij->rsj", vm["q"][...], vm["state"][...].reshape(requests, LANES, LANES),
        preferred_element_type=F32,
    )
    dotted = lambda a, b: jnp.sum(a * b, 1, keepdims=True)
    o1 = decay * read[:, 0, :] + dotted(q1, k1) * v1
    o2 = decay * decay * read[:, 1, :] + decay * (dotted(q2, k1) * v1) + dotted(q2, k2) * v2
    out = jnp.concatenate([o1, o2], 0)
    normed = out * lax.rsqrt(jnp.mean(out * out, 1, keepdims=True) + 1e-6) * vm["hg"][...]
    loads("wo").wait()
    projected = dot(normed.astype(BF16), vm["wo"][...])
    halves = [
        jnp.concatenate(
            [projected[:, (2 * a + s) * piece : (2 * a + s + 1) * piece] for a in range(depth)], 1
        )
        for s in range(2)
    ]
    first = my_side == 0
    ex_src[...] = jnp.where(first, halves[1], halves[0]).astype(BF16)
    own = jnp.where(first, halves[0], halves[1])

    loads("res").wait()
    res = vm["res"][...].astype(F32)
    res = jnp.concatenate([res[:, s, :] for s in range(steps)], 0).astype(BF16)

    def placed(size, at):
        column = lax.broadcasted_iota(jnp.int32, (piece, size), 1)
        row = lax.broadcasted_iota(jnp.int32, (piece, size), 0)
        return (column == row + at * piece).astype(BF16)

    own = own + dot(res, placed(feats, my_z))

    pl.semaphore_wait(barrier, 2 * hop + experts)
    exchange = to_partner(ex_src, ex_dst, 0)
    exchange.start()

    loads("ids").wait()
    loads("gates").wait()
    row_e = lax.broadcasted_iota(jnp.int32, (experts, requests), 0).astype(F32)
    row_m = lax.broadcasted_iota(jnp.int32, (main, requests), 0).astype(F32)
    upper = (
        lax.broadcasted_iota(jnp.int32, (requests, requests), 0)
        < lax.broadcasted_iota(jnp.int32, (requests, requests), 1)
    ).astype(BF16)
    taken = jnp.zeros((experts, 1), F32)
    kinds = 1 + lane_groups
    picks = [[] for _ in range(kinds)]
    shares = [[] for _ in range(kinds)]
    for s in range(steps):
        pick = [jnp.zeros((main, requests), F32) for _ in range(kinds)]
        share = list(pick)
        for c in range(top):
            ids = vm["ids"][s, c : c + 1, :].astype(F32)
            gate = vm["gates"][s, c : c + 1, :]
            onehot = (row_e == ids).astype(F32)
            before = dot(onehot.astype(BF16), upper) + taken
            slot = jnp.sum(onehot * before, 0, keepdims=True)
            taken = taken + jnp.sum(onehot, 1, keepdims=True)
            low = slot < SLOTS
            goals = [jnp.where(low, ids * SLOTS + slot, -1.0)]
            goals += [jnp.where(low, -1.0, ids * SLOTS + j) for j in range(lane_groups)]
            for n, goal in enumerate(goals):
                hit = (row_m == goal).astype(F32)
                pick[n] = pick[n] + hit
                share[n] = share[n] + hit * gate
        for n in range(kinds):
            picks[n].append(pick[n])
            shares[n].append(share[n])
    picks = [jnp.concatenate(p, 1).astype(BF16) for p in picks]

    def split(x):
        high = x.astype(BF16)
        return jnp.concatenate([high, (x - high.astype(F32)).astype(BF16)], 1)

    shares = [split(jnp.concatenate(s, 1).T) for s in shares]
    loads("ng").wait()
    for a in range(depth):
        at = a % span * piece
        gain_v[a // span, :, at : at + piece] = jnp.where(
            first,
            vm["ng"][:, 2 * a * piece : (2 * a + 1) * piece],
            vm["ng"][:, (2 * a + 1) * piece : (2 * a + 2) * piece],
        )
    exchange.wait()
    chip = own + ex_dst[...].astype(F32)
    for c in range(chunks):
        base = c * span * per
        for j in range(lane_groups):
            at = c * wide + j * LANES
            rows = chip[:, at : at + LANES].reshape(row_tiles, 8, LANES)
            part[base + j * row_tiles : base + (j + 1) * row_tiles] = rows.astype(BF16)
        if span * per > tiles:
            part[base + tiles : base + span * per] = jnp.zeros((span * per - tiles, 8, LANES), BF16)

    direct = 2 * hop - 1

    def block(ref, z):
        return ref.at[pl.ds(z * per, per)]

    def rs_send(src, box, base, down):
        up = depth - down
        below = down <= 2 * hop
        near = jnp.where(below, down < hop, up < hop)
        step = jnp.where(below, -jnp.where(near, down, down - hop), jnp.where(near, up, up - hop))
        length = jnp.abs(step) - 1
        slot = jnp.where(
            near,
            direct + length + jnp.where(below, 0, hop - 1),
            length + jnp.where(below, 0, hop),
        )
        group = base + jnp.where(near, 2, jnp.where(below, 0, 1))
        pltpu.make_async_remote_copy(
            src_ref=block(src, z_at(-down)), dst_ref=box.at[slot], send_sem=z_send.at[base],
            recv_sem=z_recv.at[group], device_id=(my_dp, z_at(step), my_side), device_id_type=MESH,
        ).start()

    def rs_relay(src, box, out, base, side):
        first_slot, count = ((0, hop), (hop, hop - 1))[side]
        sign = (-1, 1)[side]
        held = box.at[pl.ds(first_slot, count)]
        z_wait(held, base + side).wait_recv()
        total = src[pl.ds(z_at(sign * hop) * per, per)].astype(F32)
        for n in range(count):
            total = total + box[first_slot + n].astype(F32)
        out[side] = total.astype(BF16)
        pltpu.make_async_remote_copy(
            src_ref=out.at[side], dst_ref=box.at[depth - 3 + side], send_sem=z_send.at[base],
            recv_sem=z_recv.at[base + 2], device_id=(my_dp, z_at(sign * hop), my_side),
            device_id_type=MESH,
        ).start()

    def z_wait(held, group, send=0):
        return pltpu.make_async_remote_copy(
            src_ref=held, dst_ref=held, send_sem=z_send.at[send], recv_sem=z_recv.at[group],
            device_id=partner, device_id_type=MESH,
        )

    def rs_total(src, box, base):
        z_wait(box.at[pl.ds(direct, 2 * hop)], base + 2).wait_recv()
        total = src[pl.ds(my_z * per, per)].astype(F32)
        for n in range(direct, depth - 1):
            total = total + box[n].astype(F32)
        z_wait(box, base, base).wait_send()
        return total

    downs = [n for d in range(hop, 0, -1) for n in (hop + d, depth - hop - d)]
    downs += [n for d in range(hop - 1, 0, -1) for n in (d, depth - d)]
    for down in dict.fromkeys(downs):
        rs_send(part, inbox, 0, jnp.int32(down))

    loads("wd").wait()
    for a in range(depth):
        at = a % span * piece
        wdd[a // span, :, at : at + piece] = vm["wd"][:, a, :]

    rs_relay(part, inbox, relay, 0, 0)
    rs_relay(part, inbox, relay, 0, 1)

    kd = decay * k1
    kd_hi = kd.astype(BF16).astype(F32)
    lhs = jnp.stack([kd_hi, kd - kd_hi, k2], 1).astype(BF16)
    rhs = jnp.stack([v1, v1, v2], 1).astype(BF16)
    decay2 = decay * decay
    for r in range(requests):
        outer = lax.dot_general(
            lhs[r], rhs[r], (((0,), (0,)), ((), ())), preferred_element_type=F32
        )
        state_out[r, 0] = (decay2 * vm["state"][r, 0].astype(F32) + outer).astype(BF16)

    mine = pl.ds(my_z * per, per)
    tsum[mine] = rs_total(part, inbox, 0).astype(BF16)

    def ag_copy(origin, to):
        held = block(tsum, origin)
        return pltpu.make_async_remote_copy(
            src_ref=held, dst_ref=held, send_sem=z_send.at[1], recv_sem=z_recv.at[6 + origin],
            device_id=(my_dp, to, my_side), device_id_type=MESH,
        )

    for offset in range(hop, 0, -1):
        for sign in (1, -1):
            ag_copy(my_z, z_at(sign * offset)).start()
    for sign, reach in ((1, hop), (-1, hop - 1)):
        origin = z_at(-sign * hop)
        ag_copy(origin, z_at(sign)).wait_recv()
        for offset in range(reach, 0, -1):
            ag_copy(origin, z_at(sign * offset)).start()

    for p, chunk in enumerate(near_order):
        for b in range(span):
            origin = chunk * span + b
            away = (origin - my_z + depth) % depth

            def arrive(origin=origin):
                ag_copy(origin, z_at(1)).wait_recv()

            pl.when((away != 0) & (away != hop) & (away != depth - hop))(arrive)
        cols = []
        for j in range(lane_groups):
            rows = tsum[pl.ds(chunk * span * per + j * row_tiles, row_tiles)].astype(F32)
            cols.append(rows.reshape(tokens, LANES).astype(BF16))
        last = jnp.zeros((main, LANES), F32)
        for j, col in enumerate(cols):
            disp[p, :, j] = dot(picks[0], col).reshape(experts, SLOTS, LANES).astype(BF16)
            last = last + dot(picks[1 + j], col)
        disp[p, :, lane_groups] = last.reshape(experts, SLOTS, LANES).astype(BF16)

        def go_start(i, c, p=p):
            peer = dp_peer(i)
            dp_copy(p, disp.at[p, peer], recv.at[p, i], peer).start()
            return c

        lax.fori_loop(1, experts, go_start, 0)
        recv[p, 0] = disp[p, my_dp]
        if not nearest[p]:
            resid_out[...] = lax.dot_general(
                jnp.concatenate(cols, 1), placed(wide, my_z % span),
                (((1,), (1,)), ((), ())), preferred_element_type=F32,
            ).astype(BF16)

    z_wait(inbox, 6, 1).wait_send()
    loads("wg").wait()
    loads("wu").wait()
    unpick = [
        (
            lax.broadcasted_iota(jnp.int32, (experts, main), 1)
            == lax.broadcasted_iota(jnp.int32, (experts, main), 0) * SLOTS + j
        ).astype(BF16)
        for j in range(lane_groups)
    ]
    others = pl.ds(1, experts - 1)
    gate_own = jnp.zeros((slots, hidden), F32)
    up_own = jnp.zeros((slots, hidden), F32)
    squares = jnp.zeros((slots, LANES), F32)
    for p, chunk in enumerate(near_order):
        dp_copy(p, disp.at[p, others], recv.at[p, others], dp_peer(1)).wait()
        last = recv[p, :, lane_groups].astype(F32).reshape(main, LANES).astype(BF16)
        xs = []
        for j in range(lane_groups):
            x = jnp.concatenate(
                [recv[p, :, j].astype(F32).reshape(main, LANES), dot(unpick[j], last)], 0
            )
            squares = squares + x * x
            xs.append((x * gain_v[chunk][:, j * LANES : (j + 1) * LANES]).astype(BF16))
        x = jnp.concatenate(xs, 1)
        rows = pl.ds(chunk * span, span)
        final_chunk = p == chunks - 1
        gate_own = gate_own + dot(x, vm["wg"][rows].reshape(wide, hidden))
        if final_chunk:
            gu_src[0] = gate_own.astype(BF16)
            gate_copy = to_partner(gu_src.at[0], gu_dst.at[0], 1)
            gate_copy.start()
            ss_src[...] = jnp.broadcast_to(jnp.sum(squares, 1, keepdims=True), (slots, LANES))
            ss_copy = to_partner(ss_src, ss_dst, 2)
            ss_copy.start()
        up_own = up_own + dot(x, vm["wu"][rows].reshape(wide, hidden))
    gu_src[1] = up_own.astype(BF16)
    up_copy = to_partner(gu_src.at[1], gu_dst.at[1], 3)
    up_copy.start()
    ss_copy.wait()
    scale = lax.rsqrt((ss_src[...] + ss_dst[...]) / width + 1e-6)[:, :1]
    gate_copy.wait()
    up_copy.wait()
    gate_val = (gate_own + gu_dst[0].astype(F32)) * scale
    up_val = (up_own + gu_dst[1].astype(F32)) * scale
    act = (gate_val / (1.0 + jnp.exp(-gate_val)) * up_val).astype(BF16)

    for p, chunk in enumerate(order):
        down = dot(act, wdd[chunk])
        last = jnp.zeros((main, LANES), F32)
        for j in range(lane_groups):
            col = down[:, j * LANES : (j + 1) * LANES]
            back[p, :, j] = col[:main].reshape(experts, SLOTS, LANES).astype(BF16)
            last = last + lax.dot_general(
                unpick[j], col[main:].astype(BF16), (((0,), (0,)), ((), ())),
                preferred_element_type=F32,
            )
        back[p, :, lane_groups] = last.reshape(experts, SLOTS, LANES).astype(BF16)

        def back_start(i, c, p=p):
            dp_copy(chunks + p, back.at[p, i], comb.at[p, my_dp], home(i)).start()
            return c

        lax.fori_loop(1, experts, back_start, 0)
        comb[p, my_dp] = back[p, 0]

    for p, chunk in enumerate(order):
        dp_copy(chunks + p, back.at[p, others], comb.at[p, others], dp_peer(1)).wait()
        last = comb[p, :, lane_groups].astype(F32).reshape(main, LANES).astype(BF16)
        twice = jnp.concatenate([last, last], 0)
        cols = []
        for j in range(lane_groups):
            got = comb[p, :, j].astype(F32).reshape(main, LANES).astype(BF16)
            got = jnp.concatenate([got, got], 0)
            cols.append(dot(shares[0], got) + dot(shares[1 + j], twice))
        mixed = jnp.concatenate(cols, 1)
        for b in range(span):
            lanes = [
                mixed[t * 8 : t * 8 + 8, b * piece : (b + 1) * piece] for t in range(row_tiles)
            ]
            if per * LANES > row_tiles * piece:
                lanes.append(jnp.zeros((8, per * LANES - row_tiles * piece), F32))
            packed = jnp.concatenate(lanes, 1)
            dest = chunk * span + b
            for t in range(per):
                part2[dest * per + t] = packed[:, t * LANES : (t + 1) * LANES].astype(BF16)
        for b in range(span):
            peer = chunk * span + b

            def send(peer=peer):
                pltpu.make_async_remote_copy(
                    src_ref=block(part2, peer), dst_ref=inbox2.at[my_z], send_sem=z_send.at[2],
                    recv_sem=z_recv.at[3], device_id=(my_dp, peer, my_side), device_id_type=MESH,
                ).start()

            if ahead[p]:
                send()
            else:
                pl.when(peer != my_z)(send)
    inbox2[my_z] = part2[mine]
    z_wait(inbox2.at[pl.ds(0, depth - 1)], 3, 2).wait()
    total = inbox2[0].astype(F32)
    for n in range(1, depth):
        total = total + inbox2[n].astype(F32)
    final = jnp.concatenate([total[t] for t in range(per)], 1)
    for t in range(row_tiles):
        moe_out[t * 8 : t * 8 + 8, :] = final[:, t * piece : (t + 1) * piece].astype(BF16)


def layer(mesh_shape, q, k, v, state, slopes, hg, wo, res, ng, ids, gates, wg, wu, wd):
    experts, depth = mesh_shape["dp"], mesh_shape["heads"]
    requests, steps, head = q.shape
    piece = res.shape[2]
    hidden = wg.shape[3]
    top = ids.shape[2]
    width = ng.shape[0]
    tokens = requests * steps
    feats = depth * piece
    chunks = max(1, depth // 4)
    span = depth // chunks
    wide = span * piece
    per = -(-(wide // LANES) * (tokens // 8) // span)
    slots = experts * SLOTS + experts
    tiled = (chunks, experts, wide // LANES + 1, SLOTS, LANES)
    rows_y = 4 if experts == 16 else experts
    dims = (experts, depth, chunks, rows_y, requests, steps, top, piece, hidden, width)
    operands = {
        "q": q, "k": k, "v": v, "hg": hg.reshape(1, head), "res": res, "ng": ng.reshape(1, width),
        "ids": ids.transpose(1, 2, 0), "gates": gates.transpose(1, 2, 0), "state": state, "wo": wo,
        "wg": wg[0], "wu": wu[0], "wd": wd[0],
    }
    arrays = [operands[name] for name in IN_NAMES]
    dma = pltpu.SemaphoreType.DMA
    scratch = [pltpu.VMEM(a.shape, a.dtype) for a in arrays] + [
        pltpu.VMEM((chunks, hidden, wide), BF16),
        pltpu.VMEM((tokens, feats), BF16),
        pltpu.VMEM((tokens, feats), BF16),
        pltpu.VMEM((per * depth, 8, LANES), BF16),
        pltpu.VMEM((per * depth, 8, LANES), BF16),
        pltpu.VMEM((depth - 1, per, 8, LANES), BF16),
        pltpu.VMEM((2, per, 8, LANES), BF16),
        pltpu.VMEM(tiled, BF16),
        pltpu.VMEM(tiled, BF16),
        pltpu.VMEM((chunks, 1, wide), F32),
        pltpu.VMEM((slots, LANES), F32),
        pltpu.VMEM((slots, LANES), F32),
        pltpu.VMEM((2, slots, hidden), BF16),
        pltpu.VMEM((2, slots, hidden), BF16),
        pltpu.VMEM(tiled, BF16),
        pltpu.VMEM(tiled, BF16),
        pltpu.VMEM((per * depth, 8, LANES), BF16),
        pltpu.VMEM((depth, per, 8, LANES), BF16),
        dma((len(IN_NAMES),)),
        dma((4,)),
        dma((4,)),
        dma((4,)),
        dma((6 + depth,)),
        dma((2 * chunks,)),
        dma((2 * chunks,)),
    ]
    any_spec = pl.BlockSpec(memory_space=pl.ANY)
    state_new, resid, moe = pl.pallas_call(
        functools.partial(kernel, dims),
        out_shape=(
            pltpu.VMEM(state.shape, BF16),
            pltpu.VMEM((tokens, piece), BF16),
            pltpu.VMEM((tokens, piece), BF16),
        ),
        in_specs=[any_spec] * len(arrays) + [pl.BlockSpec(memory_space=pltpu.SMEM)],
        out_specs=(
            pl.BlockSpec(memory_space=pltpu.VMEM),
            pl.BlockSpec(memory_space=pltpu.VMEM),
            pl.BlockSpec(memory_space=pltpu.VMEM),
        ),
        scratch_shapes=scratch,
        compiler_params=pltpu.CompilerParams(
            collective_id=0, has_side_effects=True, vmem_limit_bytes=56 * 1024 * 1024
        ),
        name="layer",
    )(*arrays, slopes)
    back = lambda x: x.reshape(steps, requests, piece).transpose(1, 0, 2)
    return state_new, back(resid), back(moe)


def solution(mesh):
    return jax.shard_map(
        functools.partial(layer, dict(mesh.shape)),
        mesh=mesh,
        in_specs=(
            P("dp", None, ("heads", "side")),
            P("dp", None, ("heads", "side")),
            P("dp", None, ("heads", "side")),
            P("dp", ("heads", "side"), None, None),
            P(("heads", "side")),
            P(("heads", "side")),
            P(("heads", "side"), None),
            P("dp", None, ("heads", "side")),
            P(),
            P("dp", None, None),
            P("dp", None, None),
            P("dp", None, "side", "heads"),
            P("dp", None, "side", "heads"),
            P("dp", "heads", None, "side"),
        ),
        out_specs=(
            P("dp", ("heads", "side"), None, None),
            P("dp", None, ("heads", "side")),
            P("dp", None, ("heads", "side")),
        ),
        check_vma=False,
    )
```

```python
import functools

import jax
import jax.numpy as jnp
from jax import lax
from jax.experimental import pallas as pl
from jax.experimental.pallas import tpu as pltpu
from jax.sharding import PartitionSpec as P

F32 = jnp.float32
BF16 = jnp.bfloat16
MESH = pl.DeviceIdType.MESH
SLOTS = 8
LANES = 128
IN_NAMES = ("slope", "q", "k", "v", "hg", "res", "ng", "ids", "gates", "state", "wo", "wg", "wu", "wd")


def dot(a, b):
    return jnp.dot(a, b, preferred_element_type=F32)


def kernel(dims, *refs):
    (experts, depth, chunks, rows_y, requests, steps, top, piece, hidden, width) = dims
    tokens = requests * steps
    span = depth // chunks
    wide = span * piece
    lane_groups = wide // LANES
    row_tiles = tokens // 8
    tiles = lane_groups * row_tiles
    per = -(-tiles // span)
    feats = depth * piece
    main = experts * SLOTS
    slots = main + experts
    n_in = len(IN_NAMES)
    hbm = dict(zip(IN_NAMES, refs[:n_in]))
    state_out, resid_out, moe_out = refs[n_in : n_in + 3]
    vm = dict(zip(IN_NAMES, refs[n_in + 3 : 2 * n_in + 3]))
    (
        wdd, ex_src, ex_dst, part, tsum, inbox, relay, disp, recv, gain_v,
        gu_src, gu_dst, back, comb, part2, inbox2,
        in_sem, side_send, side_recv, z_send, z_recv, dp_send, dp_recv,
    ) = refs[2 * n_in + 3 :]

    my_dp = lax.axis_index("dp")
    my_z = lax.axis_index("heads")
    my_side = lax.axis_index("side")
    partner = (my_dp, my_z, 1 - my_side)
    my_chunk = my_z // span
    ahead = [(chunks // 2 + (p + 1) // 2 * (1 - 2 * (p % 2)) + chunks) % chunks for p in range(chunks)]
    order = [(my_chunk + shift) % chunks for shift in ahead]
    nearest = sorted(range(chunks), key=lambda shift: min(shift, chunks - shift))
    near_order = [(my_chunk + shift) % chunks for shift in nearest]
    hop = depth // 4

    def z_at(offset):
        return (my_z + offset + depth) % depth

    columns = experts // rows_y

    def dp_peer(i):
        x = (my_dp // rows_y + i // rows_y) % columns
        y = (my_dp % rows_y + i % rows_y) % rows_y
        return x * rows_y + y

    def apart(i):
        x, y = i // rows_y, i % rows_y
        return min(x, columns - x) + min(y, rows_y - y)

    dp_order = sorted(range(1, experts), key=apart, reverse=True)

    def home(i):
        x = (my_dp // rows_y - i // rows_y + columns) % columns
        y = (my_dp % rows_y - i % rows_y + rows_y) % rows_y
        return x * rows_y + y

    def loads(name):
        i = IN_NAMES.index(name)
        return pltpu.make_async_copy(hbm[name], vm[name], in_sem.at[i])

    def to_partner(src, dst, i):
        return pltpu.make_async_remote_copy(
            src_ref=src, dst_ref=dst, send_sem=side_send.at[i], recv_sem=side_recv.at[i],
            device_id=partner, device_id_type=MESH,
        )

    def dp_copy(phase, src, dst, peer):
        return pltpu.make_async_remote_copy(
            src_ref=src, dst_ref=dst, send_sem=dp_send.at[phase], recv_sem=dp_recv.at[phase],
            device_id=(peer, my_z, my_side), device_id_type=MESH,
        )

    for name in ("state", "slope", "q", "k", "v", "hg", "wo", "wd", "res", "ids", "gates", "ng", "wg", "wu"):
        loads(name).start()

    barrier = pltpu.get_barrier_semaphore()

    def greet_dp(i, c):
        pl.semaphore_signal(barrier, 1, device_id=(dp_peer(i), my_z, my_side), device_id_type=MESH)
        return c

    for offset in range(hop, 0, -1):
        for sign in (1, -1):
            pl.semaphore_signal(
                barrier, 1, device_id=(my_dp, z_at(sign * offset), my_side), device_id_type=MESH
            )
    lax.fori_loop(1, experts, greet_dp, 0)
    pl.semaphore_signal(barrier, 1, device_id=partner, device_id_type=MESH)

    for name in ("slope", "q", "k", "v", "hg", "state"):
        loads(name).wait()
    decay = jnp.exp(-jnp.broadcast_to(vm["slope"][...], (1, LANES)))
    q = vm["q"][...].astype(F32)
    k = vm["k"][...].astype(F32)
    v = vm["v"][...].astype(F32)
    q1, q2 = q[:, 0, :], q[:, 1, :]
    k1, k2 = k[:, 0, :], k[:, 1, :]
    v1, v2 = v[:, 0, :], v[:, 1, :]
    read = jnp.einsum(
        "rsi,rij->rsj", vm["q"][...], vm["state"][...].reshape(requests, LANES, LANES),
        preferred_element_type=F32,
    )
    dotted = lambda a, b: jnp.sum(a * b, 1, keepdims=True)
    o1 = decay * read[:, 0, :] + dotted(q1, k1) * v1
    o2 = decay * decay * read[:, 1, :] + decay * (dotted(q2, k1) * v1) + dotted(q2, k2) * v2
    out = jnp.concatenate([o1, o2], 0)
    normed = out * lax.rsqrt(jnp.mean(out * out, 1, keepdims=True) + 1e-6) * vm["hg"][...]
    loads("wo").wait()
    projected = dot(normed.astype(BF16), vm["wo"][...])
    halves = [
        jnp.concatenate(
            [projected[:, (2 * a + s) * piece : (2 * a + s + 1) * piece] for a in range(depth)], 1
        )
        for s in range(2)
    ]
    first = my_side == 0
    ex_src[...] = jnp.where(first, halves[1], halves[0]).astype(BF16)
    own = jnp.where(first, halves[0], halves[1])

    loads("res").wait()
    res = vm["res"][...].astype(F32)
    res = jnp.concatenate([res[:, s, :] for s in range(steps)], 0).astype(BF16)

    def placed(size, at):
        column = lax.broadcasted_iota(jnp.int32, (piece, size), 1)
        row = lax.broadcasted_iota(jnp.int32, (piece, size), 0)
        return (column == row + at * piece).astype(BF16)

    pl.semaphore_wait(barrier, 2 * hop + experts)
    exchange = to_partner(ex_src, ex_dst, 0)
    exchange.start()
    own = own + dot(res, placed(feats, my_z))

    loads("ids").wait()
    loads("gates").wait()
    row_e = lax.broadcasted_iota(jnp.int32, (experts, requests), 0).astype(F32)
    row_m = lax.broadcasted_iota(jnp.int32, (main, requests), 0).astype(F32)
    upper = (
        lax.broadcasted_iota(jnp.int32, (requests, requests), 0)
        < lax.broadcasted_iota(jnp.int32, (requests, requests), 1)
    ).astype(BF16)
    taken = jnp.zeros((experts, 1), F32)
    kinds = 1 + lane_groups
    picks = [[] for _ in range(kinds)]
    shares = [[] for _ in range(kinds)]
    for s in range(steps):
        pick = [jnp.zeros((main, requests), F32) for _ in range(kinds)]
        share = list(pick)
        for c in range(top):
            ids = vm["ids"][s, c : c + 1, :].astype(F32)
            gate = vm["gates"][s, c : c + 1, :]
            onehot = (row_e == ids).astype(F32)
            before = dot(onehot.astype(BF16), upper) + taken
            slot = jnp.sum(onehot * before, 0, keepdims=True)
            taken = taken + jnp.sum(onehot, 1, keepdims=True)
            low = slot < SLOTS
            goals = [jnp.where(low, ids * SLOTS + slot, -1.0)]
            goals += [jnp.where(low, -1.0, ids * SLOTS + j) for j in range(lane_groups)]
            for n, goal in enumerate(goals):
                hit = (row_m == goal).astype(F32)
                pick[n] = pick[n] + hit
                share[n] = share[n] + hit * gate
        for n in range(kinds):
            picks[n].append(pick[n])
            shares[n].append(share[n])
    picks = [jnp.concatenate(p, 1).astype(BF16) for p in picks]

    def split(x):
        high = x.astype(BF16)
        return jnp.concatenate([high, (x - high.astype(F32)).astype(BF16)], 1)

    shares = [split(jnp.concatenate(s, 1).T) for s in shares]
    loads("ng").wait()
    for a in range(depth):
        at = a % span * piece
        gain_v[a // span, :, at : at + piece] = jnp.where(
            first,
            vm["ng"][:, 2 * a * piece : (2 * a + 1) * piece],
            vm["ng"][:, (2 * a + 1) * piece : (2 * a + 2) * piece],
        )
    exchange.wait()
    chip = own + ex_dst[...].astype(F32)
    for c in range(chunks):
        base = c * span * per
        for j in range(lane_groups):
            at = c * wide + j * LANES
            rows = chip[:, at : at + LANES].reshape(row_tiles, 8, LANES)
            part[base + j * row_tiles : base + (j + 1) * row_tiles] = rows.astype(BF16)
        if span * per > tiles:
            part[base + tiles : base + span * per] = jnp.zeros((span * per - tiles, 8, LANES), BF16)

    direct = 2 * hop - 1

    def block(ref, z):
        return ref.at[pl.ds(z * per, per)]

    def rs_send(src, box, base, down):
        up = depth - down
        below = down <= 2 * hop
        near = jnp.where(below, down < hop, up < hop)
        step = jnp.where(below, -jnp.where(near, down, down - hop), jnp.where(near, up, up - hop))
        length = jnp.abs(step) - 1
        slot = jnp.where(
            near,
            direct + length + jnp.where(below, 0, hop - 1),
            length + jnp.where(below, 0, hop),
        )
        group = base + jnp.where(near, 2, jnp.where(below, 0, 1))
        pltpu.make_async_remote_copy(
            src_ref=block(src, z_at(-down)), dst_ref=box.at[slot], send_sem=z_send.at[base],
            recv_sem=z_recv.at[group], device_id=(my_dp, z_at(step), my_side), device_id_type=MESH,
        ).start()

    def rs_relay(src, box, out, base, side):
        first_slot, count = ((0, hop), (hop, hop - 1))[side]
        sign = (-1, 1)[side]
        held = box.at[pl.ds(first_slot, count)]
        z_wait(held, base + side).wait_recv()
        total = src[pl.ds(z_at(sign * hop) * per, per)].astype(F32)
        for n in range(count):
            total = total + box[first_slot + n].astype(F32)
        out[side] = total.astype(BF16)
        pltpu.make_async_remote_copy(
            src_ref=out.at[side], dst_ref=box.at[depth - 3 + side], send_sem=z_send.at[base],
            recv_sem=z_recv.at[base + 2], device_id=(my_dp, z_at(sign * hop), my_side),
            device_id_type=MESH,
        ).start()

    def z_wait(held, group, send=0):
        return pltpu.make_async_remote_copy(
            src_ref=held, dst_ref=held, send_sem=z_send.at[send], recv_sem=z_recv.at[group],
            device_id=partner, device_id_type=MESH,
        )

    def rs_total(src, box, base):
        z_wait(box.at[pl.ds(direct, 2 * hop)], base + 2).wait_recv()
        total = src[pl.ds(my_z * per, per)].astype(F32)
        for n in range(direct, depth - 1):
            total = total + box[n].astype(F32)
        z_wait(box, base, base).wait_send()
        return total

    downs = [n for d in range(hop, 0, -1) for n in (hop + d, depth - hop - d)]
    downs += [n for d in range(hop - 1, 0, -1) for n in (d, depth - d)]
    for down in dict.fromkeys(downs):
        rs_send(part, inbox, 0, jnp.int32(down))

    loads("wd").wait()
    for a in range(depth):
        at = a % span * piece
        wdd[a // span, :, at : at + piece] = vm["wd"][:, a, :]

    rs_relay(part, inbox, relay, 0, 0)
    rs_relay(part, inbox, relay, 0, 1)

    kd = decay * k1
    kd_hi = kd.astype(BF16).astype(F32)
    lhs = jnp.stack([kd_hi, kd - kd_hi, k2], 1).astype(BF16)
    rhs = jnp.stack([v1, v1, v2], 1).astype(BF16)
    decay2 = decay * decay
    for r in range(requests):
        outer = lax.dot_general(
            lhs[r], rhs[r], (((0,), (0,)), ((), ())), preferred_element_type=F32
        )
        state_out[r, 0] = (decay2 * vm["state"][r, 0].astype(F32) + outer).astype(BF16)

    mine = pl.ds(my_z * per, per)
    tsum[mine] = rs_total(part, inbox, 0).astype(BF16)

    def ag_copy(origin, to):
        held = block(tsum, origin)
        return pltpu.make_async_remote_copy(
            src_ref=held, dst_ref=held, send_sem=z_send.at[1], recv_sem=z_recv.at[6 + origin],
            device_id=(my_dp, to, my_side), device_id_type=MESH,
        )

    for offset in range(hop, 0, -1):
        for sign in (1, -1):
            ag_copy(my_z, z_at(sign * offset)).start()
    for sign, reach in ((1, hop), (-1, hop - 1)):
        origin = z_at(-sign * hop)
        ag_copy(origin, z_at(sign)).wait_recv()
        for offset in range(reach, 0, -1):
            ag_copy(origin, z_at(sign * offset)).start()

    for p, chunk in enumerate(near_order):
        for b in range(span):
            origin = chunk * span + b
            away = (origin - my_z + depth) % depth

            def arrive(origin=origin):
                ag_copy(origin, z_at(1)).wait_recv()

            pl.when((away != 0) & (away != hop) & (away != depth - hop))(arrive)
        cols = []
        for j in range(lane_groups):
            rows = tsum[pl.ds(chunk * span * per + j * row_tiles, row_tiles)].astype(F32)
            cols.append(rows.reshape(tokens, LANES).astype(BF16))
        last = jnp.zeros((main, LANES), F32)
        for j, col in enumerate(cols):
            disp[p, :, j] = dot(picks[0], col).reshape(experts, SLOTS, LANES).astype(BF16)
            last = last + dot(picks[1 + j], col)
        disp[p, :, lane_groups] = last.reshape(experts, SLOTS, LANES).astype(BF16)

        for i in dp_order:
            peer = dp_peer(i)
            dp_copy(p, disp.at[p, peer], recv.at[p, i], peer).start()
        recv[p, 0] = disp[p, my_dp]
        if not nearest[p]:
            resid_out[...] = lax.dot_general(
                jnp.concatenate(cols, 1), placed(wide, my_z % span),
                (((1,), (1,)), ((), ())), preferred_element_type=F32,
            ).astype(BF16)

    z_wait(inbox, 6, 1).wait_send()
    loads("wg").wait()
    loads("wu").wait()
    unpick = [
        (
            lax.broadcasted_iota(jnp.int32, (experts, main), 1)
            == lax.broadcasted_iota(jnp.int32, (experts, main), 0) * SLOTS + j
        ).astype(BF16)
        for j in range(lane_groups)
    ]
    others = pl.ds(1, experts - 1)
    gate_own = jnp.zeros((slots, hidden), F32)
    up_own = jnp.zeros((slots, hidden), F32)
    squares = jnp.zeros((slots, LANES), F32)
    for p, chunk in enumerate(near_order):
        dp_copy(p, disp.at[p, others], recv.at[p, others], dp_peer(1)).wait()
        last = recv[p, :, lane_groups].astype(F32).reshape(main, LANES).astype(BF16)
        xs = []
        for j in range(lane_groups):
            x = jnp.concatenate(
                [recv[p, :, j].astype(F32).reshape(main, LANES), dot(unpick[j], last)], 0
            )
            squares = squares + x * x
            xs.append((x * gain_v[chunk][:, j * LANES : (j + 1) * LANES]).astype(BF16))
        x = jnp.concatenate(xs, 1)
        rows = pl.ds(chunk * span, span)
        final_chunk = p == chunks - 1
        gate_own = gate_own + dot(x, vm["wg"][rows].reshape(wide, hidden))
        if final_chunk:
            spare = gu_src.shape[2] - hidden
            squares = jnp.sum(squares, 1, keepdims=True)
            high = squares.astype(BF16).astype(F32)
            gu_src[0, :, :hidden] = gate_own.astype(BF16)
            gu_src[0, :, hidden:] = jnp.broadcast_to(high, (slots, spare)).astype(BF16)
            gate_copy = to_partner(gu_src.at[0], gu_dst.at[0], 1)
            gate_copy.start()
            gu_src[1, :, hidden:] = jnp.broadcast_to(squares - high, (slots, spare)).astype(BF16)
        up_own = up_own + dot(x, vm["wu"][rows].reshape(wide, hidden))
    gu_src[1, :, :hidden] = up_own.astype(BF16)
    up_copy = to_partner(gu_src.at[1], gu_dst.at[1], 2)
    up_copy.start()
    gate_copy.wait()
    up_copy.wait()
    for half in range(2):
        squares = squares + gu_dst[half, :, hidden : hidden + 1].astype(F32)
    scale = lax.rsqrt(squares / width + 1e-6)
    gate_val = (gate_own + gu_dst[0, :, :hidden].astype(F32)) * scale
    up_val = (up_own + gu_dst[1, :, :hidden].astype(F32)) * scale
    act = (gate_val / (1.0 + jnp.exp(-gate_val)) * up_val).astype(BF16)

    for p, chunk in enumerate(order):
        down = dot(act, wdd[chunk])
        last = jnp.zeros((main, LANES), F32)
        for j in range(lane_groups):
            col = down[:, j * LANES : (j + 1) * LANES]
            back[p, :, j] = col[:main].reshape(experts, SLOTS, LANES).astype(BF16)
            last = last + lax.dot_general(
                unpick[j], col[main:].astype(BF16), (((0,), (0,)), ((), ())),
                preferred_element_type=F32,
            )
        back[p, :, lane_groups] = last.reshape(experts, SLOTS, LANES).astype(BF16)

        for i in dp_order:
            dp_copy(chunks + p, back.at[p, i], comb.at[p, my_dp], home(i)).start()
        comb[p, my_dp] = back[p, 0]

    for p, chunk in enumerate(order):
        dp_copy(chunks + p, back.at[p, others], comb.at[p, others], dp_peer(1)).wait()
        last = comb[p, :, lane_groups].astype(F32).reshape(main, LANES).astype(BF16)
        twice = jnp.concatenate([last, last], 0)
        cols = []
        for j in range(lane_groups):
            got = comb[p, :, j].astype(F32).reshape(main, LANES).astype(BF16)
            got = jnp.concatenate([got, got], 0)
            cols.append(dot(shares[0], got) + dot(shares[1 + j], twice))
        mixed = jnp.concatenate(cols, 1)
        for b in range(span):
            lanes = [
                mixed[t * 8 : t * 8 + 8, b * piece : (b + 1) * piece] for t in range(row_tiles)
            ]
            if per * LANES > row_tiles * piece:
                lanes.append(jnp.zeros((8, per * LANES - row_tiles * piece), F32))
            packed = jnp.concatenate(lanes, 1)
            dest = chunk * span + b
            for t in range(per):
                part2[dest * per + t] = packed[:, t * LANES : (t + 1) * LANES].astype(BF16)
        for b in range(span):
            peer = chunk * span + b

            def send(peer=peer):
                pltpu.make_async_remote_copy(
                    src_ref=block(part2, peer), dst_ref=inbox2.at[my_z], send_sem=z_send.at[2],
                    recv_sem=z_recv.at[3], device_id=(my_dp, peer, my_side), device_id_type=MESH,
                ).start()

            if ahead[p]:
                send()
            else:
                pl.when(peer != my_z)(send)
    inbox2[my_z] = part2[mine]
    z_wait(inbox2.at[pl.ds(0, depth - 1)], 3, 2).wait()
    total = inbox2[0].astype(F32)
    for n in range(1, depth):
        total = total + inbox2[n].astype(F32)
    final = jnp.concatenate([total[t] for t in range(per)], 1)
    for t in range(row_tiles):
        moe_out[t * 8 : t * 8 + 8, :] = final[:, t * piece : (t + 1) * piece].astype(BF16)


def layer(mesh_shape, q, k, v, state, slopes, hg, wo, res, ng, ids, gates, wg, wu, wd):
    experts, depth = mesh_shape["dp"], mesh_shape["heads"]
    requests, steps, head = q.shape
    piece = res.shape[2]
    hidden = wg.shape[3]
    top = ids.shape[2]
    width = ng.shape[0]
    tokens = requests * steps
    feats = depth * piece
    chunks = max(1, depth // 4)
    span = depth // chunks
    wide = span * piece
    per = -(-(wide // LANES) * (tokens // 8) // span)
    slots = experts * SLOTS + experts
    tiled = (chunks, experts, wide // LANES + 1, SLOTS, LANES)
    rows_y = 4 if experts == 16 else experts
    dims = (experts, depth, chunks, rows_y, requests, steps, top, piece, hidden, width)
    operands = {
        "slope": slopes.reshape(1, 1), "q": q, "k": k, "v": v, "hg": hg.reshape(1, head), "res": res, "ng": ng.reshape(1, width),
        "ids": ids.transpose(1, 2, 0), "gates": gates.transpose(1, 2, 0), "state": state, "wo": wo,
        "wg": wg[0], "wu": wu[0], "wd": wd[0],
    }
    arrays = [operands[name] for name in IN_NAMES]
    dma = pltpu.SemaphoreType.DMA
    scratch = [pltpu.VMEM(a.shape, a.dtype) for a in arrays] + [
        pltpu.VMEM((chunks, hidden, wide), BF16),
        pltpu.VMEM((tokens, feats), BF16),
        pltpu.VMEM((tokens, feats), BF16),
        pltpu.VMEM((per * depth, 8, LANES), BF16),
        pltpu.VMEM((per * depth, 8, LANES), BF16),
        pltpu.VMEM((depth - 1, per, 8, LANES), BF16),
        pltpu.VMEM((2, per, 8, LANES), BF16),
        pltpu.VMEM(tiled, BF16),
        pltpu.VMEM(tiled, BF16),
        pltpu.VMEM((chunks, 1, wide), F32),
        pltpu.VMEM((2, slots, (hidden // LANES + 1) * LANES), BF16),
        pltpu.VMEM((2, slots, (hidden // LANES + 1) * LANES), BF16),
        pltpu.VMEM(tiled, BF16),
        pltpu.VMEM(tiled, BF16),
        pltpu.VMEM((per * depth, 8, LANES), BF16),
        pltpu.VMEM((depth, per, 8, LANES), BF16),
        dma((len(IN_NAMES),)),
        dma((3,)),
        dma((3,)),
        dma((3,)),
        dma((6 + depth,)),
        dma((2 * chunks,)),
        dma((2 * chunks,)),
    ]
    any_spec = pl.BlockSpec(memory_space=pl.ANY)
    state_new, resid, moe = pl.pallas_call(
        functools.partial(kernel, dims),
        out_shape=(
            pltpu.VMEM(state.shape, BF16),
            pltpu.VMEM((tokens, piece), BF16),
            pltpu.VMEM((tokens, piece), BF16),
        ),
        in_specs=[any_spec] * len(arrays),
        out_specs=(
            pl.BlockSpec(memory_space=pltpu.VMEM),
            pl.BlockSpec(memory_space=pltpu.VMEM),
            pl.BlockSpec(memory_space=pltpu.VMEM),
        ),
        scratch_shapes=scratch,
        compiler_params=pltpu.CompilerParams(
            collective_id=0, has_side_effects=True, vmem_limit_bytes=56 * 1024 * 1024
        ),
        name="layer",
    )(*arrays)
    back = lambda x: x.reshape(steps, requests, piece).transpose(1, 0, 2)
    return state_new, back(resid), back(moe)


def solution(mesh):
    return jax.shard_map(
        functools.partial(layer, dict(mesh.shape)),
        mesh=mesh,
        in_specs=(
            P("dp", None, ("heads", "side")),
            P("dp", None, ("heads", "side")),
            P("dp", None, ("heads", "side")),
            P("dp", ("heads", "side"), None, None),
            P(("heads", "side")),
            P(("heads", "side")),
            P(("heads", "side"), None),
            P("dp", None, ("heads", "side")),
            P(),
            P("dp", None, None),
            P("dp", None, None),
            P("dp", None, "side", "heads"),
            P("dp", None, "side", "heads"),
            P("dp", "heads", None, "side"),
        ),
        out_specs=(
            P("dp", ("heads", "side"), None, None),
            P("dp", None, ("heads", "side")),
            P("dp", None, ("heads", "side")),
        ),
        check_vma=False,
    )
```

```python
import functools

import jax
import jax.numpy as jnp
from jax import lax
from jax.experimental import pallas as pl
from jax.experimental.pallas import tpu as pltpu
from jax.sharding import PartitionSpec as P

F32 = jnp.float32
BF16 = jnp.bfloat16
MESH = pl.DeviceIdType.MESH
SLOTS = 8
LANES = 128
IN_NAMES = ("slope", "q", "k", "v", "hg", "res", "ng", "ids", "gates", "state", "wo", "wg", "wu", "wd")


def dot(a, b):
    return jnp.dot(a, b, preferred_element_type=F32)


def kernel(dims, *refs):
    (experts, depth, chunks, rows_y, requests, steps, top, piece, hidden, width) = dims
    tokens = requests * steps
    span = depth // chunks
    wide = span * piece
    lane_groups = wide // LANES
    row_tiles = tokens // 8
    tiles = lane_groups * row_tiles
    per = -(-tiles // span)
    feats = depth * piece
    main = experts * SLOTS
    slots = main + experts
    n_in = len(IN_NAMES)
    hbm = dict(zip(IN_NAMES, refs[:n_in]))
    state_out, resid_out, moe_out = refs[n_in : n_in + 3]
    vm = dict(zip(IN_NAMES, refs[n_in + 3 : 2 * n_in + 3]))
    (
        wdd, ex_src, ex_dst, part, tsum, inbox, relay, disp, recv, gain_v,
        gu_src, gu_dst, back, comb, part2, inbox2,
        in_sem, side_send, side_recv, z_send, z_recv, dp_send, dp_recv,
    ) = refs[2 * n_in + 3 :]

    my_dp = lax.axis_index("dp")
    my_z = lax.axis_index("heads")
    my_side = lax.axis_index("side")
    partner = (my_dp, my_z, 1 - my_side)
    my_chunk = my_z // span
    ahead = [(chunks // 2 + (p + 1) // 2 * (1 - 2 * (p % 2)) + chunks) % chunks for p in range(chunks)]
    order = [(my_chunk + shift) % chunks for shift in ahead]
    nearest = sorted(range(chunks), key=lambda shift: min(shift, chunks - shift))
    near_order = [(my_chunk + shift) % chunks for shift in nearest]
    hop = depth // 4

    def z_at(offset):
        return (my_z + offset + depth) % depth

    columns = experts // rows_y

    def dp_peer(i):
        x = (my_dp // rows_y + i // rows_y) % columns
        y = (my_dp % rows_y + i % rows_y) % rows_y
        return x * rows_y + y

    def apart(i):
        x, y = i // rows_y, i % rows_y
        return min(x, columns - x) + min(y, rows_y - y)

    dp_order = sorted(range(1, experts), key=apart, reverse=True)

    def home(i):
        x = (my_dp // rows_y - i // rows_y + columns) % columns
        y = (my_dp % rows_y - i % rows_y + rows_y) % rows_y
        return x * rows_y + y

    def loads(name):
        i = IN_NAMES.index(name)
        return pltpu.make_async_copy(hbm[name], vm[name], in_sem.at[i])

    def to_partner(src, dst, i):
        return pltpu.make_async_remote_copy(
            src_ref=src, dst_ref=dst, send_sem=side_send.at[i], recv_sem=side_recv.at[i],
            device_id=partner, device_id_type=MESH,
        )

    def dp_copy(phase, src, dst, peer):
        return pltpu.make_async_remote_copy(
            src_ref=src, dst_ref=dst, send_sem=dp_send.at[phase], recv_sem=dp_recv.at[phase],
            device_id=(peer, my_z, my_side), device_id_type=MESH,
        )

    for name in ("state", "slope", "q", "k", "v", "hg", "wo", "wd", "res", "ids", "gates", "ng", "wg", "wu"):
        loads(name).start()

    barrier = pltpu.get_barrier_semaphore()

    def greet_dp(i, c):
        pl.semaphore_signal(barrier, 1, device_id=(dp_peer(i), my_z, my_side), device_id_type=MESH)
        return c

    for offset in range(hop, 0, -1):
        for sign in (1, -1):
            pl.semaphore_signal(
                barrier, 1, device_id=(my_dp, z_at(sign * offset), my_side), device_id_type=MESH
            )
    lax.fori_loop(1, experts, greet_dp, 0)
    pl.semaphore_signal(barrier, 1, device_id=partner, device_id_type=MESH)

    for name in ("slope", "q", "k", "v", "hg", "state"):
        loads(name).wait()
    decay = jnp.exp(-jnp.broadcast_to(vm["slope"][...], (1, LANES)))
    q = vm["q"][...].astype(F32)
    k = vm["k"][...].astype(F32)
    v = vm["v"][...].astype(F32)
    q1, q2 = q[:, 0, :], q[:, 1, :]
    k1, k2 = k[:, 0, :], k[:, 1, :]
    v1, v2 = v[:, 0, :], v[:, 1, :]
    read = jnp.einsum(
        "rsi,rij->rsj", vm["q"][...], vm["state"][...].reshape(requests, LANES, LANES),
        preferred_element_type=F32,
    )
    dotted = lambda a, b: jnp.sum(a * b, 1, keepdims=True)
    o1 = decay * read[:, 0, :] + dotted(q1, k1) * v1
    o2 = decay * decay * read[:, 1, :] + decay * (dotted(q2, k1) * v1) + dotted(q2, k2) * v2
    out = jnp.concatenate([o1, o2], 0)
    normed = out * lax.rsqrt(jnp.mean(out * out, 1, keepdims=True) + 1e-6) * vm["hg"][...]
    loads("wo").wait()
    projected = dot(normed.astype(BF16), vm["wo"][...])
    halves = [
        jnp.concatenate(
            [projected[:, (2 * a + s) * piece : (2 * a + s + 1) * piece] for a in range(depth)], 1
        )
        for s in range(2)
    ]
    first = my_side == 0
    ex_src[...] = jnp.where(first, halves[1], halves[0]).astype(BF16)
    own = jnp.where(first, halves[0], halves[1])

    loads("res").wait()
    res = vm["res"][...].astype(F32)
    res = jnp.concatenate([res[:, s, :] for s in range(steps)], 0).astype(BF16)

    def placed(size, at):
        column = lax.broadcasted_iota(jnp.int32, (piece, size), 1)
        row = lax.broadcasted_iota(jnp.int32, (piece, size), 0)
        return (column == row + at * piece).astype(BF16)

    pl.semaphore_wait(barrier, 2 * hop + experts)
    exchange = to_partner(ex_src, ex_dst, 0)
    exchange.start()
    own = own + dot(res, placed(feats, my_z))

    loads("ids").wait()
    loads("gates").wait()
    row_e = lax.broadcasted_iota(jnp.int32, (experts, requests), 0).astype(F32)
    row_m = lax.broadcasted_iota(jnp.int32, (main, requests), 0).astype(F32)
    upper = (
        lax.broadcasted_iota(jnp.int32, (requests, requests), 0)
        < lax.broadcasted_iota(jnp.int32, (requests, requests), 1)
    ).astype(BF16)
    taken = jnp.zeros((experts, 1), F32)
    kinds = 1 + lane_groups
    picks = [[] for _ in range(kinds)]
    shares = [[] for _ in range(kinds)]
    for s in range(steps):
        pick = [jnp.zeros((main, requests), F32) for _ in range(kinds)]
        share = list(pick)
        for c in range(top):
            ids = vm["ids"][s, c : c + 1, :].astype(F32)
            gate = vm["gates"][s, c : c + 1, :]
            onehot = (row_e == ids).astype(F32)
            before = dot(onehot.astype(BF16), upper) + taken
            slot = jnp.sum(onehot * before, 0, keepdims=True)
            taken = taken + jnp.sum(onehot, 1, keepdims=True)
            low = slot < SLOTS
            goals = [jnp.where(low, ids * SLOTS + slot, -1.0)]
            goals += [jnp.where(low, -1.0, ids * SLOTS + j) for j in range(lane_groups)]
            for n, goal in enumerate(goals):
                hit = (row_m == goal).astype(F32)
                pick[n] = pick[n] + hit
                share[n] = share[n] + hit * gate
        for n in range(kinds):
            picks[n].append(pick[n])
            shares[n].append(share[n])
    picks = [jnp.concatenate(p, 1).astype(BF16) for p in picks]

    def split(x):
        high = x.astype(BF16)
        return jnp.concatenate([high, (x - high.astype(F32)).astype(BF16)], 1)

    shares = [split(jnp.concatenate(s, 1).T) for s in shares]
    loads("ng").wait()
    for a in range(depth):
        at = a % span * piece
        gain_v[a // span, :, at : at + piece] = jnp.where(
            first,
            vm["ng"][:, 2 * a * piece : (2 * a + 1) * piece],
            vm["ng"][:, (2 * a + 1) * piece : (2 * a + 2) * piece],
        )
    exchange.wait()
    chip = own + ex_dst[...].astype(F32)
    for c in range(chunks):
        base = c * span * per
        for j in range(lane_groups):
            at = c * wide + j * LANES
            rows = chip[:, at : at + LANES].reshape(row_tiles, 8, LANES)
            part[base + j * row_tiles : base + (j + 1) * row_tiles] = rows.astype(BF16)
        if span * per > tiles:
            part[base + tiles : base + span * per] = jnp.zeros((span * per - tiles, 8, LANES), BF16)

    direct = 2 * hop - 1

    def block(ref, z):
        return ref.at[pl.ds(z * per, per)]

    def rs_send(src, box, base, down):
        up = depth - down
        below = down <= 2 * hop
        near = jnp.where(below, down < hop, up < hop)
        step = jnp.where(below, -jnp.where(near, down, down - hop), jnp.where(near, up, up - hop))
        length = jnp.abs(step) - 1
        slot = jnp.where(
            near,
            direct + length + jnp.where(below, 0, hop - 1),
            length + jnp.where(below, 0, hop),
        )
        group = base + jnp.where(near, 2, jnp.where(below, 0, 1))
        pltpu.make_async_remote_copy(
            src_ref=block(src, z_at(-down)), dst_ref=box.at[slot], send_sem=z_send.at[base],
            recv_sem=z_recv.at[group], device_id=(my_dp, z_at(step), my_side), device_id_type=MESH,
        ).start()

    def rs_relay(src, box, out, base, side):
        first_slot, count = ((0, hop), (hop, hop - 1))[side]
        sign = (-1, 1)[side]
        held = box.at[pl.ds(first_slot, count)]
        z_wait(held, base + side).wait_recv()
        total = src[pl.ds(z_at(sign * hop) * per, per)].astype(F32)
        for n in range(count):
            total = total + box[first_slot + n].astype(F32)
        out[side] = total.astype(BF16)
        pltpu.make_async_remote_copy(
            src_ref=out.at[side], dst_ref=box.at[depth - 3 + side], send_sem=z_send.at[base],
            recv_sem=z_recv.at[base + 2], device_id=(my_dp, z_at(sign * hop), my_side),
            device_id_type=MESH,
        ).start()

    def z_wait(held, group, send=0):
        return pltpu.make_async_remote_copy(
            src_ref=held, dst_ref=held, send_sem=z_send.at[send], recv_sem=z_recv.at[group],
            device_id=partner, device_id_type=MESH,
        )

    def rs_total(src, box, base):
        z_wait(box.at[pl.ds(direct, 2 * hop)], base + 2).wait_recv()
        total = src[pl.ds(my_z * per, per)].astype(F32)
        for n in range(direct, depth - 1):
            total = total + box[n].astype(F32)
        z_wait(box, base, base).wait_send()
        return total

    downs = [n for d in range(hop, 0, -1) for n in (hop + d, depth - hop - d)]
    downs += [n for d in range(hop - 1, 0, -1) for n in (d, depth - d)]
    for down in dict.fromkeys(downs):
        rs_send(part, inbox, 0, jnp.int32(down))

    rs_relay(part, inbox, relay, 0, 0)
    rs_relay(part, inbox, relay, 0, 1)

    loads("wd").wait()
    for a in range(depth):
        at = a % span * piece
        wdd[a // span, :, at : at + piece] = vm["wd"][:, a, :]

    kd = decay * k1
    kd_hi = kd.astype(BF16).astype(F32)
    lhs = jnp.stack([kd_hi, kd - kd_hi, k2], 1).astype(BF16)
    rhs = jnp.stack([v1, v1, v2], 1).astype(BF16)
    decay2 = decay * decay
    for r in range(requests):
        outer = lax.dot_general(
            lhs[r], rhs[r], (((0,), (0,)), ((), ())), preferred_element_type=F32
        )
        state_out[r, 0] = (decay2 * vm["state"][r, 0].astype(F32) + outer).astype(BF16)

    mine = pl.ds(my_z * per, per)
    tsum[mine] = rs_total(part, inbox, 0).astype(BF16)

    def ag_copy(origin, to):
        held = block(tsum, origin)
        return pltpu.make_async_remote_copy(
            src_ref=held, dst_ref=held, send_sem=z_send.at[1], recv_sem=z_recv.at[6 + origin],
            device_id=(my_dp, to, my_side), device_id_type=MESH,
        )

    for offset in range(hop, 0, -1):
        for sign in (1, -1):
            ag_copy(my_z, z_at(sign * offset)).start()
    for sign, reach in ((1, hop), (-1, hop - 1)):
        origin = z_at(-sign * hop)
        ag_copy(origin, z_at(sign)).wait_recv()
        for offset in range(reach, 0, -1):
            ag_copy(origin, z_at(sign * offset)).start()

    for p, chunk in enumerate(near_order):
        for b in range(span):
            origin = chunk * span + b
            away = (origin - my_z + depth) % depth

            def arrive(origin=origin):
                ag_copy(origin, z_at(1)).wait_recv()

            pl.when((away != 0) & (away != hop) & (away != depth - hop))(arrive)
        cols = []
        for j in range(lane_groups):
            rows = tsum[pl.ds(chunk * span * per + j * row_tiles, row_tiles)].astype(F32)
            cols.append(rows.reshape(tokens, LANES).astype(BF16))
        last = jnp.zeros((main, LANES), F32)
        for j, col in enumerate(cols):
            disp[p, :, j] = dot(picks[0], col).reshape(experts, SLOTS, LANES).astype(BF16)
            last = last + dot(picks[1 + j], col)
        disp[p, :, lane_groups] = last.reshape(experts, SLOTS, LANES).astype(BF16)

        for i in dp_order:
            peer = dp_peer(i)
            dp_copy(p, disp.at[p, peer], recv.at[p, i], peer).start()
        recv[p, 0] = disp[p, my_dp]
        if not nearest[p]:
            resid_out[...] = lax.dot_general(
                jnp.concatenate(cols, 1), placed(wide, my_z % span),
                (((1,), (1,)), ((), ())), preferred_element_type=F32,
            ).astype(BF16)

    z_wait(inbox, 6, 1).wait_send()
    loads("wg").wait()
    loads("wu").wait()
    unpick = [
        (
            lax.broadcasted_iota(jnp.int32, (experts, main), 1)
            == lax.broadcasted_iota(jnp.int32, (experts, main), 0) * SLOTS + j
        ).astype(BF16)
        for j in range(lane_groups)
    ]
    others = pl.ds(1, experts - 1)
    gate_own = jnp.zeros((slots, hidden), F32)
    up_own = jnp.zeros((slots, hidden), F32)
    squares = jnp.zeros((slots, LANES), F32)
    for p, chunk in enumerate(near_order):
        dp_copy(p, disp.at[p, others], recv.at[p, others], dp_peer(1)).wait()
        last = recv[p, :, lane_groups].astype(F32).reshape(main, LANES).astype(BF16)
        xs = []
        for j in range(lane_groups):
            x = jnp.concatenate(
                [recv[p, :, j].astype(F32).reshape(main, LANES), dot(unpick[j], last)], 0
            )
            squares = squares + x * x
            xs.append((x * gain_v[chunk][:, j * LANES : (j + 1) * LANES]).astype(BF16))
        x = jnp.concatenate(xs, 1)
        rows = pl.ds(chunk * span, span)
        final_chunk = p == chunks - 1
        gate_own = gate_own + dot(x, vm["wg"][rows].reshape(wide, hidden))
        if final_chunk:
            spare = gu_src.shape[2] - hidden
            squares = jnp.sum(squares, 1, keepdims=True)
            high = squares.astype(BF16).astype(F32)
            gu_src[0, :, :hidden] = gate_own.astype(BF16)
            gu_src[0, :, hidden:] = jnp.broadcast_to(high, (slots, spare)).astype(BF16)
            gate_copy = to_partner(gu_src.at[0], gu_dst.at[0], 1)
            gate_copy.start()
            gu_src[1, :, hidden:] = jnp.broadcast_to(squares - high, (slots, spare)).astype(BF16)
        up_own = up_own + dot(x, vm["wu"][rows].reshape(wide, hidden))
    gu_src[1, :, :hidden] = up_own.astype(BF16)
    up_copy = to_partner(gu_src.at[1], gu_dst.at[1], 2)
    up_copy.start()
    gate_copy.wait()
    up_copy.wait()
    for half in range(2):
        squares = squares + gu_dst[half, :, hidden : hidden + 1].astype(F32)
    scale = lax.rsqrt(squares / width + 1e-6)
    gate_val = (gate_own + gu_dst[0, :, :hidden].astype(F32)) * scale
    up_val = (up_own + gu_dst[1, :, :hidden].astype(F32)) * scale
    act = (gate_val / (1.0 + jnp.exp(-gate_val)) * up_val).astype(BF16)

    for p, chunk in enumerate(order):
        down = dot(act, wdd[chunk])
        last = jnp.zeros((main, LANES), F32)
        for j in range(lane_groups):
            col = down[:, j * LANES : (j + 1) * LANES]
            back[p, :, j] = col[:main].reshape(experts, SLOTS, LANES).astype(BF16)
            last = last + lax.dot_general(
                unpick[j], col[main:].astype(BF16), (((0,), (0,)), ((), ())),
                preferred_element_type=F32,
            )
        back[p, :, lane_groups] = last.reshape(experts, SLOTS, LANES).astype(BF16)

        for i in dp_order:
            dp_copy(chunks + p, back.at[p, i], comb.at[p, my_dp], home(i)).start()
        comb[p, my_dp] = back[p, 0]

    for p, chunk in enumerate(order):
        dp_copy(chunks + p, back.at[p, others], comb.at[p, others], dp_peer(1)).wait()
        last = comb[p, :, lane_groups].astype(F32).reshape(main, LANES).astype(BF16)
        twice = jnp.concatenate([last, last], 0)
        cols = []
        for j in range(lane_groups):
            got = comb[p, :, j].astype(F32).reshape(main, LANES).astype(BF16)
            got = jnp.concatenate([got, got], 0)
            cols.append(dot(shares[0], got) + dot(shares[1 + j], twice))
        mixed = jnp.concatenate(cols, 1)
        for b in range(span):
            lanes = [
                mixed[t * 8 : t * 8 + 8, b * piece : (b + 1) * piece] for t in range(row_tiles)
            ]
            if per * LANES > row_tiles * piece:
                lanes.append(jnp.zeros((8, per * LANES - row_tiles * piece), F32))
            packed = jnp.concatenate(lanes, 1)
            dest = chunk * span + b
            for t in range(per):
                part2[dest * per + t] = packed[:, t * LANES : (t + 1) * LANES].astype(BF16)
        for b in range(span):
            peer = chunk * span + b

            def send(peer=peer):
                pltpu.make_async_remote_copy(
                    src_ref=block(part2, peer), dst_ref=inbox2.at[my_z], send_sem=z_send.at[2],
                    recv_sem=z_recv.at[3], device_id=(my_dp, peer, my_side), device_id_type=MESH,
                ).start()

            if ahead[p]:
                send()
            else:
                pl.when(peer != my_z)(send)
    inbox2[my_z] = part2[mine]
    z_wait(inbox2.at[pl.ds(0, depth - 1)], 3, 2).wait()
    total = inbox2[0].astype(F32)
    for n in range(1, depth):
        total = total + inbox2[n].astype(F32)
    final = jnp.concatenate([total[t] for t in range(per)], 1)
    for t in range(row_tiles):
        moe_out[t * 8 : t * 8 + 8, :] = final[:, t * piece : (t + 1) * piece].astype(BF16)


def layer(mesh_shape, q, k, v, state, slopes, hg, wo, res, ng, ids, gates, wg, wu, wd):
    experts, depth = mesh_shape["dp"], mesh_shape["heads"]
    requests, steps, head = q.shape
    piece = res.shape[2]
    hidden = wg.shape[3]
    top = ids.shape[2]
    width = ng.shape[0]
    tokens = requests * steps
    feats = depth * piece
    chunks = max(1, depth // 4)
    span = depth // chunks
    wide = span * piece
    per = -(-(wide // LANES) * (tokens // 8) // span)
    slots = experts * SLOTS + experts
    tiled = (chunks, experts, wide // LANES + 1, SLOTS, LANES)
    rows_y = 4 if experts == 16 else experts
    dims = (experts, depth, chunks, rows_y, requests, steps, top, piece, hidden, width)
    operands = {
        "slope": slopes.reshape(1, 1), "q": q, "k": k, "v": v, "hg": hg.reshape(1, head), "res": res, "ng": ng.reshape(1, width),
        "ids": ids.transpose(1, 2, 0), "gates": gates.transpose(1, 2, 0), "state": state, "wo": wo,
        "wg": wg[0], "wu": wu[0], "wd": wd[0],
    }
    arrays = [operands[name] for name in IN_NAMES]
    dma = pltpu.SemaphoreType.DMA
    scratch = [pltpu.VMEM(a.shape, a.dtype) for a in arrays] + [
        pltpu.VMEM((chunks, hidden, wide), BF16),
        pltpu.VMEM((tokens, feats), BF16),
        pltpu.VMEM((tokens, feats), BF16),
        pltpu.VMEM((per * depth, 8, LANES), BF16),
        pltpu.VMEM((per * depth, 8, LANES), BF16),
        pltpu.VMEM((depth - 1, per, 8, LANES), BF16),
        pltpu.VMEM((2, per, 8, LANES), BF16),
        pltpu.VMEM(tiled, BF16),
        pltpu.VMEM(tiled, BF16),
        pltpu.VMEM((chunks, 1, wide), F32),
        pltpu.VMEM((2, slots, (hidden // LANES + 1) * LANES), BF16),
        pltpu.VMEM((2, slots, (hidden // LANES + 1) * LANES), BF16),
        pltpu.VMEM(tiled, BF16),
        pltpu.VMEM(tiled, BF16),
        pltpu.VMEM((per * depth, 8, LANES), BF16),
        pltpu.VMEM((depth, per, 8, LANES), BF16),
        dma((len(IN_NAMES),)),
        dma((3,)),
        dma((3,)),
        dma((3,)),
        dma((6 + depth,)),
        dma((2 * chunks,)),
        dma((2 * chunks,)),
    ]
    any_spec = pl.BlockSpec(memory_space=pl.ANY)
    state_new, resid, moe = pl.pallas_call(
        functools.partial(kernel, dims),
        out_shape=(
            pltpu.VMEM(state.shape, BF16),
            pltpu.VMEM((tokens, piece), BF16),
            pltpu.VMEM((tokens, piece), BF16),
        ),
        in_specs=[any_spec] * len(arrays),
        out_specs=(
            pl.BlockSpec(memory_space=pltpu.VMEM),
            pl.BlockSpec(memory_space=pltpu.VMEM),
            pl.BlockSpec(memory_space=pltpu.VMEM),
        ),
        scratch_shapes=scratch,
        compiler_params=pltpu.CompilerParams(
            collective_id=0, has_side_effects=True, vmem_limit_bytes=56 * 1024 * 1024
        ),
        name="layer",
    )(*arrays)
    back = lambda x: x.reshape(steps, requests, piece).transpose(1, 0, 2)
    return state_new, back(resid), back(moe)


def solution(mesh):
    return jax.shard_map(
        functools.partial(layer, dict(mesh.shape)),
        mesh=mesh,
        in_specs=(
            P("dp", None, ("heads", "side")),
            P("dp", None, ("heads", "side")),
            P("dp", None, ("heads", "side")),
            P("dp", ("heads", "side"), None, None),
            P(("heads", "side")),
            P(("heads", "side")),
            P(("heads", "side"), None),
            P("dp", None, ("heads", "side")),
            P(),
            P("dp", None, None),
            P("dp", None, None),
            P("dp", None, "side", "heads"),
            P("dp", None, "side", "heads"),
            P("dp", "heads", None, "side"),
        ),
        out_specs=(
            P("dp", ("heads", "side"), None, None),
            P("dp", None, ("heads", "side")),
            P("dp", None, ("heads", "side")),
        ),
        check_vma=False,
    )
```
